32 devices in a mesh: frames: 8 (over z, y), band: 4 (over x, core).
Axes of the slice: x: 2, y: 2, z: 4, core: 2. Of those that a mesh axis runs over, the one named last changes fastest.
Arguments:
- tokens: bfloat16 [16, 1024, 1024], P('frames', 'band'), may hold values from -6 to 6
- norm_space: float32 [1024], replicated, may hold values from 0.5 to 1.5
- query_space: bfloat16 [1024, 1024], replicated, may hold values from -0.1875 to 0.1875
- keyval_space: bfloat16 [1024, 512], replicated, may hold values from -0.1875 to 0.1875
- out_space: bfloat16 [1024, 1024], replicated, may hold values from -0.1875 to 0.1875
- qk_space: float32 [2, 64], replicated, may hold values from 0.7 to 7
- norm_time: float32 [1024], replicated, may hold values from 0.5 to 1.5
- query_time: bfloat16 [1024, 1024], replicated, may hold values from -0.1875 to 0.1875
- keyval_time: bfloat16 [1024, 512], replicated, may hold values from -0.1875 to 0.1875
- out_time: bfloat16 [1024, 1024], replicated, may hold values from -0.1875 to 0.1875
- qk_time: float32 [2, 64], replicated, may hold values from 0.7 to 7
Outputs:
- mixed: bfloat16 [16, 1024, 1024], P('frames', 'band')
The draws below stay inside these ranges and needn't reach their ends.
All inputs are finite; a program needn't handle non-finite values.
Results may differ from the reference program's by a relative error of at most 0.025.
The reference program's roundings to bfloat16 on the way count: a program that leaves them out, or rounds other values in their place, can miss the bound.
Values may be sent and summed in bfloat16 or wider, within the bound.
No kernel may reach another device: no remote copies, remote signals or barrier semaphores. Data moves between devices by JAX's collectives and lax.ppermute only.
A program may use at most 128 MiB of HBM per device.

```python
import jax
import jax.numpy as jnp
from jax import lax

D = 1024
HEADS = 16
KV_HEADS = 4
HEAD_DIM = 64
PATCHES = 1024
FRAMES = 16


def draw_qk_space(key, part):
    sub_key = jax.random.fold_in(key, 11)
    return jax.random.uniform(sub_key, (2, HEAD_DIM), jnp.float32, 0.7, 1.4)


def draw_qk_time(key, part):
    sub_key = jax.random.fold_in(key, 23)
    return jax.random.uniform(sub_key, (2, HEAD_DIM), jnp.float32, 0.7, 1.4)


def steps_of(stream_key, shape, split, low, high):
    def one(dim, shards_of):
        draws = jax.random.uniform(jax.random.fold_in(jax.random.fold_in(stream_key, 6), dim), (shards_of,), jnp.float32, low / len(split), high / len(split))
        return jnp.repeat(jnp.exp(draws), shape[dim] // shards_of).reshape((-1,) + (1,) * (len(shape) - dim - 1))

    loudness = one(*split[0])
    for cut in split[1:]:
        loudness = loudness * one(*cut)
    return loudness


def noise(stream_key, extent, deviation, most, cuts=(), kind=jnp.bfloat16):
    result = deviation * jax.random.normal(stream_key, extent, jnp.float32)
    if cuts:
        result = result * steps_of(stream_key, extent, cuts, -0.22, 0.18)
    return jnp.clip(result, -most, most).astype(kind)


def setup_inputs(seed: int = 0) -> dict:
    key_list = jax.random.split(jax.random.key(seed), 12)
    tokens = noise(key_list[0], (FRAMES, PATCHES, D), 1.0, 6.0, ((0, 8), (1, 4)))
    norm_space = jnp.clip(jax.random.uniform(key_list[1], (D,), jnp.float32, 0.5, 1.5), 0.5, 1.5)
    query_space = noise(key_list[2], (D, HEADS * HEAD_DIM), D ** -0.5, 0.1875)
    keyval_space = noise(key_list[3], (D, 2 * KV_HEADS * HEAD_DIM), D ** -0.5, 0.1875)
    out_space = noise(key_list[4], (HEADS * HEAD_DIM, D), (HEADS * HEAD_DIM) ** -0.5, 0.1875)
    qk_space = draw_qk_space(jax.random.fold_in(key_list[11], 71), 0)
    norm_time = jnp.clip(jax.random.uniform(key_list[6], (D,), jnp.float32, 0.5, 1.5), 0.5, 1.5)
    query_time = noise(key_list[7], (D, HEADS * HEAD_DIM), D ** -0.5, 0.1875)
    keyval_time = noise(key_list[8], (D, 2 * KV_HEADS * HEAD_DIM), D ** -0.5, 0.1875)
    out_time = noise(key_list[9], (HEADS * HEAD_DIM, D), (HEADS * HEAD_DIM) ** -0.5, 0.1875)
    qk_time = draw_qk_time(jax.random.fold_in(key_list[11], 71), 0)
    return dict(tokens=tokens, norm_space=norm_space, query_space=query_space, keyval_space=keyval_space, out_space=out_space, qk_space=qk_space, norm_time=norm_time, query_time=query_time, keyval_time=keyval_time, out_time=out_time, qk_time=qk_time)


def rms_rows(values, gain):
    values = values.astype(jnp.float32)
    scaled = lax.rsqrt(lax.optimization_barrier(jnp.mean(values * values, axis=-1, keepdims=True)) + 1e-06)
    return values * scaled * gain

def project(hidden, w_query, w_keyval, qk_gain):
    row_count = hidden.shape[0]
    queries = jnp.dot(hidden, w_query, preferred_element_type=jnp.float32)
    keyval = jnp.dot(hidden, w_keyval, preferred_element_type=jnp.float32)
    queries = rms_rows(queries.reshape(row_count, HEADS, HEAD_DIM), qk_gain[0])
    key_part = keyval[:, :KV_HEADS * HEAD_DIM].reshape(row_count, KV_HEADS, HEAD_DIM)
    key_rows = rms_rows(key_part, qk_gain[1])
    values = keyval[:, KV_HEADS * HEAD_DIM:]
    return (queries.reshape(row_count, -1).astype(jnp.bfloat16), key_rows.reshape(row_count, -1).astype(jnp.bfloat16), values.astype(jnp.bfloat16))

def attend(queries, key_rows, values, causal_mask):
    query_count = queries.shape[0]
    key_count = key_rows.shape[0]
    groups = HEADS // KV_HEADS
    grouped = queries.astype(jnp.float32).reshape(query_count, KV_HEADS, groups, HEAD_DIM)
    key_heads = key_rows.astype(jnp.float32).reshape(key_count, KV_HEADS, HEAD_DIM)
    value_heads = values.astype(jnp.float32).reshape(key_count, KV_HEADS, HEAD_DIM)
    scores = jnp.einsum('nkgd,mkd->kgnm', grouped, key_heads) * HEAD_DIM ** (-0.5)
    if causal_mask is not None:
        scores = jnp.where(causal_mask, scores, -jnp.inf)
    largest = lax.optimization_barrier(jnp.max(scores, axis=-1, keepdims=True))
    expos = jnp.exp(scores - largest)
    totals = lax.optimization_barrier(jnp.sum(expos, axis=-1))
    weights = expos.astype(jnp.bfloat16).astype(jnp.float32)
    summed = jnp.einsum('kgnm,mkd->nkgd', weights, value_heads)
    summed = summed / jnp.transpose(totals, (2, 0, 1))[..., None]
    return summed.reshape(query_count, HEADS * HEAD_DIM).astype(jnp.bfloat16)

def reference(tokens, norm_space, query_space, keyval_space, out_space, qk_space, norm_time, query_time, keyval_time, out_time, qk_time):

    def space_frame(frame_tokens):
        normed = rms_rows(frame_tokens, norm_space).astype(jnp.bfloat16)
        queries, key_rows, values = project(normed, query_space, keyval_space, qk_space)
        attended = attend(queries, key_rows, values, None)
        update = jnp.dot(attended, out_space, preferred_element_type=jnp.float32)
        stream = (frame_tokens.astype(jnp.float32) + update).astype(jnp.bfloat16)
        normed_time = rms_rows(stream, norm_time).astype(jnp.bfloat16)
        time_q, time_k, time_v = project(normed_time, query_time, keyval_time, qk_time)
        return (stream, time_q, time_k, time_v)
    stream, time_q, time_k, time_v = lax.map(space_frame, tokens)
    frame_count = tokens.shape[0]
    order = jnp.arange(frame_count, dtype=jnp.int32)
    causal_mask = order[:, None] >= order[None, :]
    block_rows = 256

    def regroup(array):
        moved = jnp.swapaxes(array, 0, 1)
        return moved.reshape(PATCHES // block_rows, block_rows, frame_count, array.shape[-1])

    def time_block(pieces):
        block_q, block_k, block_v = pieces
        return jax.vmap(lambda qq, kk, vv: attend(qq, kk, vv, causal_mask))(block_q, block_k, block_v)
    attended = lax.map(time_block, (regroup(time_q), regroup(time_k), regroup(time_v)))
    attended = jnp.swapaxes(attended.reshape(PATCHES, frame_count, HEADS * HEAD_DIM), 0, 1)

    def out_frame(pieces):
        frame_stream, frame_att = pieces
        update = jnp.dot(frame_att, out_time, preferred_element_type=jnp.float32)
        return (frame_stream.astype(jnp.float32) + update).astype(jnp.bfloat16)
    return lax.map(out_frame, (stream, attended))
```

```python
import functools

import jax
import jax.numpy as jnp
from jax import lax
from jax.experimental import pallas as pl
from jax.experimental.pallas import tpu as pltpu
from jax.sharding import PartitionSpec as P

EPS = 1e-06
LOG2E = 1.4426950408889634
BF16 = jnp.bfloat16
F32 = jnp.float32
LANES = 128
VMEM_LIMIT = 58 * 1024 * 1024


def dot(a, b):
    return jnp.dot(a, b, preferred_element_type=F32)


def dot_t(a, b):
    return lax.dot_general(a, b, (((1,), (1,)), ((), ())), preferred_element_type=F32)


def row_rms(x, gain):
    x = x.astype(F32)
    return x * lax.rsqrt(jnp.mean(x * x, axis=-1, keepdims=True) + EPS) * gain


def head_mask(width, head):
    shift = head.bit_length() - 1
    i = lax.broadcasted_iota(jnp.int32, (width, width), 0)
    j = lax.broadcasted_iota(jnp.int32, (width, width), 1)
    return jnp.where((i >> shift) == (j >> shift), 1.0, 0.0).astype(BF16)


def head_rms(x, gain, ones, head):
    width = ones.shape[0]
    parts = []
    for c in range(0, x.shape[1], width):
        v = x[:, c : c + width]
        sq = v * v
        hi = sq.astype(BF16)
        lo = (sq - hi.astype(F32)).astype(BF16)
        total = dot(hi, ones) + dot(lo, ones)
        parts.append(v * lax.rsqrt(total * (1.0 / head) + EPS) * gain[:, c : c + width])
    return parts


def twice(tile, head):
    lane = lax.broadcasted_iota(jnp.int32, tile.shape, 1)
    other = pltpu.roll(tile, head, 1)
    low = lane < head
    return jnp.where(low, tile, other), jnp.where(low, other, tile)


def store_queries(parts, q_ref, rows, head):
    scale = LOG2E * head**-0.5
    at = 0
    for part in parts:
        rounded = part.astype(BF16).astype(F32) * scale
        for t in range(0, part.shape[1], 2 * head):
            for one in twice(rounded[:, t : t + 2 * head], head):
                hi = one.astype(BF16).astype(F32)
                lane = lax.broadcasted_iota(jnp.int32, one.shape, 1)
                q_ref[rows, at : at + 2 * head] = jnp.where(lane < head, hi, one - hi).astype(BF16)
                at += 2 * head


def store_doubled(x, out_ref, rows, head):
    at = 0
    for t in range(0, x.shape[1], 2 * head):
        for one in twice(x[:, t : t + 2 * head].astype(F32), head):
            out_ref[rows, at : at + 2 * head] = one.astype(BF16)
            at += 2 * head


def softmax_out(scores, values):
    largest = jnp.max(scores, axis=-1, keepdims=True)
    expos = jnp.exp2(scores - largest)
    total = jnp.sum(expos, axis=-1, keepdims=True)
    return dot(expos.astype(BF16), values) / total


def merge_heads(out, rows, head):
    tiles = []
    for j in range(0, out.shape[0] // rows, 2):
        a = out[j * rows : (j + 1) * rows]
        b = out[(j + 1) * rows : (j + 2) * rows]
        lane = lax.broadcasted_iota(jnp.int32, a.shape, 1)
        tiles.append(jnp.where(lane < head, a, b))
    return jnp.concatenate(tiles, axis=1).astype(BF16)


def keyval_kernel(head, x_ref, norm_ref, w_ref, gain_ref, normed_ref, kv_ref):
    normed = row_rms(x_ref[...], norm_ref[...]).astype(BF16)
    normed_ref[...] = normed
    kv = dot(normed, w_ref[...])
    half = kv.shape[1] // 2
    ones = head_mask(min(256, half), head)
    parts = head_rms(kv[:, :half], gain_ref[...], ones, head)
    kv_ref[:, :half] = jnp.concatenate(parts, axis=1).astype(BF16)
    kv_ref[:, half:] = kv[:, half:].astype(BF16)


def query_kernel(head, x_ref, w_ref, gain_ref, q_ref):
    ones = head_mask(min(256, w_ref.shape[1]), head)
    q = dot(x_ref[...], w_ref[...])
    parts = head_rms(q, gain_ref[...], ones, head)
    store_queries(parts, q_ref, slice(None), head)


def space_kernel(head, first, pieces, *refs):
    (q_ref, x_ref, w_ref, norm_ref), refs = refs[:4], refs[4:]
    kv_refs, (stream_ref, timed_ref, k_buf, v_buf, att) = refs[:pieces], refs[pieces:]
    frames, rows = stream_ref.shape[0], stream_ref.shape[1]
    kv_heads = kv_refs[0].shape[2] // (2 * head)
    heads = q_ref.shape[2] // (2 * head)
    group = heads // kv_heads
    half = kv_heads * head
    wide = 2 * head

    def frame(f, carry):
        for i, ref in enumerate(kv_refs):
            n = ref.shape[1]
            store_doubled(ref[f, :, :half], k_buf, slice(i * n, (i + 1) * n), head)
            store_doubled(ref[f, :, half:], v_buf, slice(i * n, (i + 1) * n), head)

        def key_head(g, c):
            lanes = pl.ds(pl.multiple_of(g * wide, wide), wide)
            keys, values = k_buf[:, lanes], v_buf[:, lanes]
            for j in range(0, group, 2):
                outs = []
                for i in (j, j + 1):
                    at = pl.multiple_of((g * group + i) * wide, wide)
                    q = q_ref[f, first : first + rows, pl.ds(at, wide)]
                    outs.append(softmax_out(dot_t(q, keys), values))
                lane = lax.broadcasted_iota(jnp.int32, outs[0].shape, 1)
                at = pl.multiple_of(g * group * head + j * head, wide)
                att[:, pl.ds(at, wide)] = jnp.where(lane < head, outs[0], outs[1]).astype(BF16)
            return c

        lax.fori_loop(0, kv_heads, key_head, 0)
        update = dot(att[...], w_ref[...])
        stream = (x_ref[f, first : first + rows].astype(F32) + update).astype(BF16)
        stream_ref[f] = stream
        timed_ref[f] = row_rms(stream, norm_ref[...]).astype(BF16)
        return carry

    lax.fori_loop(0, frames, frame, 0)


def time_kernel(head, frames_here, spots, mix_ref, x_ref, wq_ref, wkv_ref, gq_ref, gk_ref, out_ref, q_buf, k_buf, v_buf):
    rows = x_ref.shape[0]
    half = wkv_ref.shape[1] // 2
    kv_heads = half // head
    group = wq_ref.shape[1] // head // kv_heads
    wide = 2 * head
    x = x_ref[...]
    ones = head_mask(min(256, half), head)
    kv = dot(x, wkv_ref[...])
    keys = jnp.concatenate(head_rms(kv[:, :half], gk_ref[...], ones, head), axis=1).astype(BF16)
    store_doubled(keys, k_buf, slice(None), head)
    store_doubled(kv[:, half:].astype(BF16), v_buf, slice(None), head)
    store_queries(head_rms(dot(x, wq_ref[...]), gq_ref[...], ones, head), q_buf, slice(None), head)

    def place(axis):
        n = lax.broadcasted_iota(jnp.int32, (rows, rows), axis)
        source = n // (frames_here * spots)
        frame = (source ^ mix_ref[0]) * frames_here + (n // spots) % frames_here
        return frame, n % spots

    (frame_q, spot_q), (frame_k, spot_k) = place(0), place(1)
    seen = (spot_q == spot_k) & (frame_q >= frame_k)

    def key_head(g, c):
        lanes = pl.ds(pl.multiple_of(g * wide, wide), wide)
        keys, values = k_buf[:, lanes], v_buf[:, lanes]
        for j in range(0, group, 2):
            outs = []
            for i in (j, j + 1):
                at = pl.multiple_of((g * group + i) * wide, wide)
                scores = dot_t(q_buf[:, pl.ds(at, wide)], keys)
                outs.append(softmax_out(jnp.where(seen, scores, -1e30), values))
            lane = lax.broadcasted_iota(jnp.int32, outs[0].shape, 1)
            at = pl.multiple_of(g * group * head + j * head, wide)
            out_ref[:, pl.ds(at, wide)] = jnp.where(lane < head, outs[0], outs[1]).astype(BF16)
        return c

    lax.fori_loop(0, kv_heads, key_head, 0)


def final_kernel(a_ref, x_ref, w_ref, out_ref):
    out_ref[...] = (x_ref[...].astype(F32) + dot(a_ref[...], w_ref[...])).astype(BF16)


def call(kernel, outs, flops, scratch=(), smem=()):
    single = not isinstance(outs, (list, tuple))
    shapes = [outs] if single else list(outs)

    def run(*args):
        moved = sum(a.size * a.dtype.itemsize for a in args) + sum(s.size * s.dtype.itemsize for s in shapes)
        vmem = pl.BlockSpec(memory_space=pltpu.VMEM)
        specs = [pl.BlockSpec(memory_space=pltpu.SMEM) if i in smem else vmem for i in range(len(args))]
        result = pl.pallas_call(
            kernel,
            out_shape=shapes,
            in_specs=specs,
            out_specs=[vmem] * len(shapes),
            scratch_shapes=list(scratch),
            compiler_params=pltpu.CompilerParams(vmem_limit_bytes=VMEM_LIMIT),
            cost_estimate=pl.CostEstimate(flops=int(flops), bytes_accessed=int(moved), transcendentals=0),
        )(*args)
        return result[0] if single else result

    return run


def shaped(*dims):
    return jax.ShapeDtypeStruct(dims, BF16)


def gather_all(x, axis, size):
    pieces = [x]
    step = size // 2
    while step:
        pieces += [lax.ppermute(p, axis, [(i, i ^ step) for i in range(size)]) for p in pieces]
        step //= 2
    return pieces


def make_body(mesh):
    frame_devices, band_devices = mesh.shape["frames"], mesh.shape["band"]

    def body(tokens, norm_space, query_space, keyval_space, out_space, qk_space, norm_time, query_time, keyval_time, out_time, qk_time):
        frames, rows, width = tokens.shape
        head = qk_space.shape[1]
        q_width, half = query_space.shape[1], keyval_space.shape[1] // 2
        heads, kv_heads = q_width // head, half // head
        flat = frames * rows
        gains = [jnp.tile(g[i], n)[None] for g in (qk_space, qk_time) for i, n in ((0, heads), (1, kv_heads))]

        normed, kv = call(functools.partial(keyval_kernel, head), [shaped(flat, width), shaped(flat, 2 * half)], 4 * flat * width * half)(
            tokens.reshape(flat, width), norm_space[None], keyval_space, gains[1]
        )
        all_kv = gather_all(kv.reshape(frames, rows, 2 * half), "band", band_devices)
        queries = call(functools.partial(query_kernel, head), shaped(flat, 2 * q_width), 2 * flat * width * q_width)(normed, query_space, gains[0])
        queries = queries.reshape(frames, rows, 2 * q_width)

        chunks = 2
        part = rows // chunks
        spots = part // frame_devices
        mix = jnp.zeros((1,), jnp.int32)
        keys = rows * band_devices
        outs = []
        for c in range(chunks):
            stream, timed = call(
                functools.partial(space_kernel, head, c * part, len(all_kv)),
                [shaped(frames, part, width), shaped(frames, part, width)],
                frames * part * (16 * keys * q_width + 2 * q_width * width),
                [pltpu.VMEM((keys, 2 * half), BF16), pltpu.VMEM((keys, 2 * half), BF16), pltpu.VMEM((part, q_width), BF16)],
            )(queries, tokens, out_space, norm_time[None], *all_kv)
            sent = timed.reshape(frames, frame_devices, spots, width).swapaxes(0, 1)
            moved = lax.all_to_all(sent, "frames", 0, 0)
            n = frame_devices * frames * spots
            att = call(
                functools.partial(time_kernel, head, frames, spots),
                shaped(n, q_width),
                2 * n * width * (q_width + 2 * half) + 16 * n * n * q_width,
                [pltpu.VMEM((n, 2 * q_width), BF16), pltpu.VMEM((n, 2 * half), BF16), pltpu.VMEM((n, 2 * half), BF16)],
                smem=(0,),
            )(mix, moved.reshape(n, width), query_time, keyval_time, gains[2], gains[3])
            back = lax.all_to_all(att.reshape(frame_devices, frames, spots, q_width), "frames", 0, 0)
            back = back.swapaxes(0, 1).reshape(frames * part, q_width)
            mixed = call(final_kernel, shaped(frames * part, width), 2 * frames * part * width * q_width)(
                back, stream.reshape(frames * part, width), out_time
            )
            outs.append(mixed.reshape(frames, part, width))
        return jnp.concatenate(outs, axis=1)

    return body


def solution(mesh):
    placed = (P("frames", "band", None),) + (P(),) * 10
    return jax.shard_map(make_body(mesh), mesh=mesh, in_specs=placed, out_specs=P("frames", "band", None), check_vma=False)
```

```python
import functools

import jax
import jax.numpy as jnp
from jax import lax
from jax.experimental import pallas as pl
from jax.experimental.pallas import tpu as pltpu
from jax.sharding import PartitionSpec as P


EPS = 1e-06
LOG2E = 1.4426950408889634
BF16 = jnp.bfloat16
F32 = jnp.float32


def dot(a, b):
    return jnp.dot(a, b, preferred_element_type=F32)


def row_rms(x, gain):
    x = x.astype(F32)
    return x * lax.rsqrt(jnp.mean(x * x, axis=-1, keepdims=True) + EPS) * gain


def column(row):
    n = row.shape[1]
    i = lax.broadcasted_iota(jnp.int32, (n, n), 0)
    j = lax.broadcasted_iota(jnp.int32, (n, n), 1)
    return jnp.sum(jnp.where(i == j, row, 0.0), axis=1, keepdims=True)


def feature_rms(x, gain):
    n = gain.shape[0]
    y = x.reshape(x.shape[0] // n, n, x.shape[1])
    total = jnp.sum(y * y, axis=1, keepdims=True)
    return (y * lax.rsqrt(total * (1.0 / n) + EPS) * gain[None]).reshape(x.shape)


def at(start, size):
    return pl.ds(pl.multiple_of(start, size), size)


def padded(q, odd):
    zero = jnp.zeros_like(q)
    return jnp.concatenate([zero, q] if odd else [q, zero], axis=0)


def query_columns(q_ref, lead, g, group, head, odd):
    heads = [q_ref[(*lead, at((g * group + i) * head, head), slice(None))] for i in range(group)]
    return jnp.concatenate([padded(q, odd) for q in heads], axis=1)


def keyval_kernel(x_ref, norm_ref, w_ref, gain_ref, normed_ref, kv_ref):
    frames, rows = kv_ref.shape[0], x_ref.shape[0] // kv_ref.shape[0]
    half = w_ref.shape[1] // 2
    gain = column(gain_ref[1:2, :])
    for f in range(frames):
        part = slice(f * rows, (f + 1) * rows)
        normed = row_rms(x_ref[part], norm_ref[...]).astype(BF16)
        normed_ref[part] = normed
        kv = dot(normed, w_ref[...]).T
        kv_ref[f, :rows] = feature_rms(kv[:half], gain).T.astype(BF16)
        kv_ref[f, rows:] = kv[half:].astype(BF16)


def over_key_heads(frames, kv_heads, score, finish, bufs):
    pairs = kv_heads // 2
    total = frames * pairs

    def split(step):
        return step // pairs, (step % pairs) * 2

    score(0, 0, False, bufs[0])

    def step(n, carry):
        f, g = split(n)
        f_next, g_next = split(jnp.minimum(n + 1, total - 1))
        score(f, g + 1, True, bufs[1])
        finish(f, g, bufs[0])
        score(f_next, g_next, False, bufs[0])
        finish(f, g + 1, bufs[1])
        return carry

    lax.fori_loop(0, total, step, 0)


def near_kernel(head, chunks, pieces, x_ref, w_ref, gain_ref, *refs):
    kv_refs, refs = refs[:pieces], refs[pieces:]
    (q_refs, o_refs, ml_refs), (q_buf, s0, s1) = (refs[i * chunks : (i + 1) * chunks] for i in range(3)), refs[3 * chunks :]
    frames, rows = kv_refs[0].shape[0], x_ref.shape[0] // kv_refs[0].shape[0]
    half = kv_refs[0].shape[2]
    heads, kv_heads = w_ref.shape[1] // head, half // head
    group, part, wide = heads // kv_heads, rows // chunks, 2 * head
    gain = column(gain_ref[0:1, :])
    for f in range(frames):
        q = dot(x_ref[f * rows : (f + 1) * rows], w_ref[...]).T
        q = (feature_rms(q, gain).astype(BF16).astype(F32) * head**-0.5).astype(BF16)
        q_buf[f] = q
        for c in range(chunks):
            q_refs[c][f] = q[:, c * part : (c + 1) * part]

    def score(f, g, odd, buf):
        keys = jnp.concatenate([ref[f, :rows, at((g // 2) * wide, wide)] for ref in kv_refs], axis=0)
        buf[...] = dot(keys, query_columns(q_buf, (f,), g, group, head, odd))

    def finish(f, g, buf):
        s = buf[...]
        largest = jnp.max(s, axis=0, keepdims=True)
        e = jnp.exp2((s - largest) * LOG2E)
        total = jnp.sum(e, axis=0, keepdims=True)
        values = jnp.concatenate([ref[f, at(rows + g * head, head), :] for ref in kv_refs], axis=1)
        out = dot(values, e.astype(BF16))
        for i in range(group):
            h = g * group + i
            for c in range(chunks):
                lanes = slice(i * rows + c * part, i * rows + (c + 1) * part)
                o_refs[c][f, at(h * head, head), :] = out[:, lanes]
                ml_refs[c][f, pl.ds(h, 1), :] = largest[:, lanes]
                ml_refs[c][f, pl.ds(heads + h, 1), :] = total[:, lanes]

    over_key_heads(frames, kv_heads, score, finish, (s0, s1))


def far_kernel(head, spots, pieces, q_ref, o_ref, ml_ref, x_ref, norm_ref, w_hbm, *refs):
    kv_refs, (stream_ref, timed_ref, att, s0, s1, w_ref, sem) = refs[:pieces], refs[pieces:]
    copy = pltpu.make_async_copy(w_hbm, w_ref, sem)
    copy.start()
    frames, rows, part = q_ref.shape[0], kv_refs[0].shape[1] - kv_refs[0].shape[2], q_ref.shape[2]
    half = kv_refs[0].shape[2]
    heads, kv_heads = q_ref.shape[1] // head, half // head
    group, wide = heads // kv_heads, 2 * head

    def score(f, g, odd, buf):
        keys = jnp.concatenate([ref[f, :rows, at((g // 2) * wide, wide)] for ref in kv_refs], axis=0)
        buf[...] = dot(keys, query_columns(q_ref, (f,), g, group, head, odd))

    def finish(f, g, buf):
        s = buf[...]
        before = jnp.concatenate([ml_ref[f, pl.ds(g * group + i, 1), :] for i in range(group)], axis=1)
        total = jnp.concatenate([ml_ref[f, pl.ds(heads + g * group + i, 1), :] for i in range(group)], axis=1)
        out = jnp.concatenate([o_ref[f, at((g * group + i) * head, head), :] for i in range(group)], axis=1)
        largest = jnp.maximum(before, jnp.max(s, axis=0, keepdims=True))
        scale = jnp.exp2((before - largest) * LOG2E)
        e = jnp.exp2((s - largest) * LOG2E)
        total = total * scale + jnp.sum(e, axis=0, keepdims=True)
        values = jnp.concatenate([ref[f, at(rows + g * head, head), :] for ref in kv_refs], axis=1)
        out = ((out * scale + dot(values, e.astype(BF16))) / total).astype(BF16)
        for i in range(group):
            att[f, at((g * group + i) * head, head), :] = out[:, i * part : (i + 1) * part]

    over_key_heads(frames, kv_heads, score, finish, (s0, s1))
    copy.wait()
    for f in range(frames):
        update = dot(att[f].T, w_ref[...])
        stream = (x_ref[f].astype(F32) + update).astype(BF16)
        timed = row_rms(stream, norm_ref[...]).astype(BF16)
        if spots:
            for d in range(part // spots):
                stream_ref[d, f] = stream[d * spots : (d + 1) * spots]
                timed_ref[d, f] = timed[d * spots : (d + 1) * spots]
        else:
            stream_ref[f] = stream
            timed_ref[f] = timed


def time_kernel(head, spots, x_ref, wkv_ref, wq_hbm, gain_ref, out_ref, wq_ref, q_buf, k_buf, v_buf, bias, att, sem):
    copy = pltpu.make_async_copy(wq_hbm, wq_ref, sem)
    copy.start()
    rows = x_ref.shape[0]
    half = wkv_ref.shape[1] // 2
    kv_heads = half // head
    group, wide = wq_ref.shape[1] // head // kv_heads, 2 * head
    x = x_ref[...]
    kv = dot(x, wkv_ref[...]).T
    k_buf[...] = feature_rms(kv[:half], column(gain_ref[1:2, :])).T.astype(BF16)
    v_buf[...] = kv[half:].astype(BF16)

    def place(axis):
        n = lax.broadcasted_iota(jnp.int32, (rows, rows), axis)
        return n // spots, n % spots

    (frame_k, spot_k), (frame_q, spot_q) = place(0), place(1)
    bias[...] = jnp.where((spot_q == spot_k) & (frame_q >= frame_k), 0.0, -1e30)
    copy.wait()
    q = feature_rms(dot(x, wq_ref[...]).T, column(gain_ref[0:1, :]))
    q_buf[...] = (q.astype(BF16).astype(F32) * head**-0.5).astype(BF16)
    for g in range(kv_heads):
        keys = k_buf[:, (g // 2) * wide : (g // 2 + 1) * wide]
        s = dot(keys, query_columns(q_buf, (), g, group, head, g % 2 == 1))
        s = jnp.concatenate([s[:, i * rows : (i + 1) * rows] + bias[...] for i in range(group)], axis=1)
        largest = jnp.max(s, axis=0, keepdims=True)
        e = jnp.exp2((s - largest) * LOG2E)
        total = jnp.sum(e, axis=0, keepdims=True)
        out = (dot(v_buf[g * head : (g + 1) * head], e.astype(BF16)) / total).astype(BF16)
        for i in range(group):
            h = g * group + i
            att[h * head : (h + 1) * head] = out[:, i * rows : (i + 1) * rows]
    out_ref[...] = att[...].T


def final_kernel(spots, a_ref, x_ref, w_ref, *refs):
    out_ref = refs[-1]
    mixed = (x_ref[...].astype(F32) + dot(a_ref[...], w_ref[...])).astype(BF16)
    frames, part = out_ref.shape[0], out_ref.shape[1]
    for f in range(frames):
        if spots:
            for d in range(part // spots):
                first = (d * frames + f) * spots
                out_ref[f, d * spots : (d + 1) * spots] = mixed[first : first + spots]
        else:
            out_ref[f] = mixed[f * part : (f + 1) * part]


def call(kernel, args, outs, flops, scratch=(), anywhere=(), blocks={}, out_blocks={}, alias={}):
    moved = sum(a.size * a.dtype.itemsize for a in args) + sum(s.size * s.dtype.itemsize for s in outs)

    def spec(shape, block):
        if block is None:
            return pl.BlockSpec(shape, lambda i: (0,) * len(shape))
        return pl.BlockSpec(*block)

    in_specs = [pl.BlockSpec(memory_space=pl.ANY) if i in anywhere else spec(a.shape, blocks.get(i)) for i, a in enumerate(args)]
    return pl.pallas_call(
        kernel,
        grid=(1,),
        out_shape=outs,
        in_specs=in_specs,
        out_specs=[spec(s.shape, out_blocks.get(i)) for i, s in enumerate(outs)],
        scratch_shapes=list(scratch),
        input_output_aliases=alias,
        compiler_params=pltpu.CompilerParams(vmem_limit_bytes=56 * 1024 * 1024),
        cost_estimate=pl.CostEstimate(flops=int(flops), bytes_accessed=int(moved), transcendentals=0),
    )(*args)


def shaped(*dims, dtype=BF16):
    return jax.ShapeDtypeStruct(dims, dtype)


def permuted(x, axis, size, bit):
    return lax.ppermute(x, axis, [(i, i ^ bit) for i in range(size)])


def make_body(mesh):
    frame_devices, band_devices = mesh.shape["frames"], mesh.shape["band"]
    chunks = 2

    def body(tokens, norm_space, query_space, keyval_space, out_space, qk_space, norm_time, query_time, keyval_time, out_time, qk_time):
        frames, rows, width = tokens.shape
        head = qk_space.shape[1]
        q_width, half = query_space.shape[1], keyval_space.shape[1] // 2
        heads = q_width // head
        flat, part = frames * rows, rows // chunks
        spots = part // frame_devices
        aligned = spots if spots % 16 == 0 else 0
        norm_space, norm_time = norm_space[None], norm_time[None]

        normed, kv = call(
            keyval_kernel,
            (tokens.reshape(flat, width), norm_space, keyval_space, qk_space),
            [shaped(flat, width), shaped(frames, rows + half, half)],
            4 * flat * width * half,
        )
        top = band_devices // 2
        far = [permuted(kv, "band", band_devices, top)]
        near, bit = [kv], top // 2
        while bit:
            near += [permuted(p, "band", band_devices, bit) for p in near]
            far += [permuted(p, "band", band_devices, bit) for p in far]
            bit //= 2

        near_keys = rows * len(near)
        outs = call(
            functools.partial(near_kernel, head, chunks, len(near)),
            (normed, query_space, qk_space, *near),
            [shaped(frames, q_width, part)] * chunks
            + [shaped(frames, q_width, part, dtype=F32)] * chunks
            + [shaped(frames, 2 * heads, part, dtype=F32)] * chunks,
            2 * flat * width * q_width + 8 * flat * near_keys * q_width,
            [pltpu.VMEM((frames, q_width, rows), BF16)] + [pltpu.VMEM((near_keys, rows * (q_width // half)), F32)] * 2,
        )
        far_keys = rows * len(far)
        mixed = None
        for c in range(chunks):
            piece = (frame_devices, frames, spots, width)
            layout = piece if aligned else (frames, part, width)
            stream, timed = call(
                functools.partial(far_kernel, head, aligned, len(far)),
                (outs[c], outs[chunks + c], outs[2 * chunks + c], tokens, norm_time, out_space, *far),
                [shaped(*layout), shaped(*layout)],
                frames * part * (8 * far_keys * q_width + 2 * q_width * width),
                [pltpu.VMEM((frames, q_width, part), BF16)]
                + [pltpu.VMEM((far_keys, part * (q_width // half)), F32)] * 2
                + [pltpu.VMEM((q_width, width), BF16), pltpu.SemaphoreType.DMA],
                anywhere=(5,),
                blocks={3: ((frames, part, width), lambda i, c=c: (0, c, 0))},
            )
            if not aligned:
                timed = timed.reshape(frames, frame_devices, spots, width).swapaxes(0, 1)
            moved = lax.all_to_all(timed, "frames", 0, 0)
            n = frame_devices * frames * spots
            (att,) = call(
                functools.partial(time_kernel, head, spots),
                (moved.reshape(n, width), keyval_time, query_time, qk_time),
                [shaped(n, q_width)],
                2 * n * width * (q_width + 2 * half) + 16 * n * n * q_width,
                [
                    pltpu.VMEM((width, q_width), BF16),
                    pltpu.VMEM((q_width, n), BF16),
                    pltpu.VMEM((n, half), BF16),
                    pltpu.VMEM((half, n), BF16),
                    pltpu.VMEM((n, n), F32),
                    pltpu.VMEM((q_width, n), BF16),
                    pltpu.SemaphoreType.DMA,
                ],
                anywhere=(2,),
            )
            back = lax.all_to_all(att.reshape(frame_devices, frames, spots, q_width), "frames", 0, 0)
            if not aligned:
                back = back.swapaxes(0, 1)
            args = (back.reshape(n, q_width), stream.reshape(n, width), out_time)
            (mixed,) = call(
                functools.partial(final_kernel, aligned),
                args if mixed is None else (*args, mixed),
                [shaped(frames, rows, width)],
                2 * n * width * q_width,
                anywhere=(3,),
                out_blocks={0: ((frames, part, width), lambda i, c=c: (0, c, 0))},
                alias={} if mixed is None else {3: 0},
            )
        return mixed

    return body


def solution(mesh):
    placed = (P("frames", "band", None),) + (P(),) * 10
    body = make_body(mesh)

    return jax.shard_map(body, mesh=mesh, in_specs=placed, out_specs=P("frames", "band", None), check_vma=False)
```

```python
import functools
import math

import jax
import jax.numpy as jnp
from jax import lax
from jax.experimental import pallas as pl
from jax.experimental.pallas import tpu as pltpu
from jax.sharding import PartitionSpec as P


EPS = 1e-06
LOG2E = 1.4426950408889634
BF16 = jnp.bfloat16
F32 = jnp.float32


def dot(a, b):
    return jnp.dot(a, b, preferred_element_type=F32)


def row_rms(x, gain):
    x = x.astype(F32)
    return x * lax.rsqrt(jnp.mean(x * x, axis=-1, keepdims=True) + EPS) * gain


def column(row):
    n = row.shape[1]
    i = lax.broadcasted_iota(jnp.int32, (n, n), 0)
    j = lax.broadcasted_iota(jnp.int32, (n, n), 1)
    return jnp.sum(jnp.where(i == j, row, 0.0), axis=1, keepdims=True)


def feature_rms(x, gain):
    n = gain.shape[0]
    y = x.reshape(x.shape[0] // n, n, x.shape[1])
    total = jnp.sum(y * y, axis=1, keepdims=True)
    return (y * lax.rsqrt(total * (1.0 / n) + EPS) * gain[None]).reshape(x.shape)


def at(start, size):
    return pl.ds(pl.multiple_of(start, size), size)


def padded(q, odd):
    zero = jnp.zeros_like(q)
    return jnp.concatenate([zero, q] if odd else [q, zero], axis=0)


def query_columns(q_ref, lead, g, group, head, odd):
    heads = [q_ref[(*lead, at((g * group + i) * head, head), slice(None))] for i in range(group)]
    return jnp.concatenate([padded(q, odd) for q in heads], axis=1)


def keyval_kernel(me_ref, x_ref, norm_ref, w_ref, gain_ref, normed_ref, kv_ref):
    frames, rows = kv_ref.shape[0], x_ref.shape[0] // kv_ref.shape[0]
    half = w_ref.shape[1] // 2
    gain = column(gain_ref[1:2, :])
    for f in range(frames):
        part = slice(f * rows, (f + 1) * rows)
        normed = row_rms(x_ref[part], norm_ref[...]).astype(BF16)
        normed_ref[part] = normed
        kv = dot(normed, w_ref[...]).T
        kv_ref[f, :rows] = feature_rms(kv[:half], gain).T.astype(BF16)
        kv_ref[f, rows:] = kv[half:].astype(BF16)


def over_key_heads(frames, kv_heads, score, finish, bufs):
    pairs = kv_heads // 2
    total = frames * pairs

    def split(step):
        return step // pairs, (step % pairs) * 2

    score(0, 0, False, bufs[0])

    def step(n, carry):
        f, g = split(n)
        f_next, g_next = split(jnp.minimum(n + 1, total - 1))
        score(f, g + 1, True, bufs[1])
        finish(f, g, bufs[0])
        score(f_next, g_next, False, bufs[0])
        finish(f, g + 1, bufs[1])
        return carry

    lax.fori_loop(0, total, step, 0)


def near_kernel(head, chunks, pieces, x_ref, w_ref, gain_ref, *refs):
    kv_refs, refs = refs[:pieces], refs[pieces:]
    (q_refs, o_refs, ml_refs), (q_buf, s0, s1) = (refs[i * chunks : (i + 1) * chunks] for i in range(3)), refs[3 * chunks :]
    frames, rows = kv_refs[0].shape[0], x_ref.shape[0] // kv_refs[0].shape[0]
    half = kv_refs[0].shape[2]
    heads, kv_heads = w_ref.shape[1] // head, half // head
    group, part, wide = heads // kv_heads, rows // chunks, 2 * head
    gain = column(gain_ref[0:1, :])
    for f in range(frames):
        q = dot(x_ref[f * rows : (f + 1) * rows], w_ref[...]).T
        q = (feature_rms(q, gain).astype(BF16).astype(F32) * head**-0.5).astype(BF16)
        q_buf[f] = q
        for c in range(chunks):
            q_refs[c][f] = q[:, c * part : (c + 1) * part]

    def score(f, g, odd, buf):
        keys = jnp.concatenate([ref[f, :rows, at((g // 2) * wide, wide)] for ref in kv_refs], axis=0)
        buf[...] = dot(keys, query_columns(q_buf, (f,), g, group, head, odd))

    def finish(f, g, buf):
        s = buf[...]
        largest = jnp.max(s, axis=0, keepdims=True)
        e = jnp.exp2((s - largest) * LOG2E)
        total = jnp.sum(e, axis=0, keepdims=True)
        values = jnp.concatenate([ref[f, at(rows + g * head, head), :] for ref in kv_refs], axis=1)
        out = dot(values, e.astype(BF16))
        for i in range(group):
            h = g * group + i
            for c in range(chunks):
                lanes = slice(i * rows + c * part, i * rows + (c + 1) * part)
                o_refs[c][f, at(h * head, head), :] = out[:, lanes]
                ml_refs[c][f, pl.ds(h, 1), :] = largest[:, lanes]
                ml_refs[c][f, pl.ds(heads + h, 1), :] = total[:, lanes]

    over_key_heads(frames, kv_heads, score, finish, (s0, s1))


def far_kernel(head, first, spots, pieces, me_ref, q_ref, o_ref, ml_ref, x_ref, norm_ref, w_ref, *refs):
    kv_refs, stream_ref, refs = refs[:pieces], refs[pieces], refs[pieces + 1 :]
    timed_refs, (att, s0, s1, timed_buf) = refs[:-4], refs[-4:]
    frames, part, half = q_ref.shape[0], q_ref.shape[2], kv_refs[0].shape[2]
    rows = kv_refs[0].shape[1] - half
    heads, kv_heads = q_ref.shape[1] // head, half // head
    group, wide = heads // kv_heads, 2 * head

    def score(f, g, odd, buf):
        keys = jnp.concatenate([ref[f, :rows, at((g // 2) * wide, wide)] for ref in kv_refs], axis=0)
        buf[...] = dot(keys, query_columns(q_ref, (f,), g, group, head, odd))

    def finish(f, g, buf):
        s = buf[...]
        before = jnp.concatenate([ml_ref[f, pl.ds(g * group + i, 1), :] for i in range(group)], axis=1)
        total = jnp.concatenate([ml_ref[f, pl.ds(heads + g * group + i, 1), :] for i in range(group)], axis=1)
        out = jnp.concatenate([o_ref[f, at((g * group + i) * head, head), :] for i in range(group)], axis=1)
        largest = jnp.maximum(before, jnp.max(s, axis=0, keepdims=True))
        scale = jnp.exp2((before - largest) * LOG2E)
        e = jnp.exp2((s - largest) * LOG2E)
        total = total * scale + jnp.sum(e, axis=0, keepdims=True)
        values = jnp.concatenate([ref[f, at(rows + g * head, head), :] for ref in kv_refs], axis=1)
        out = ((out * scale + dot(values, e.astype(BF16))) / total).astype(BF16)
        for i in range(group):
            att[f, at((g * group + i) * head, head), :] = out[:, i * part : (i + 1) * part]

    over_key_heads(frames, kv_heads, score, finish, (s0, s1))
    for f in range(frames):
        update = dot(att[f].T, w_ref[...])
        stream = (x_ref[f, first : first + part].astype(F32) + update).astype(BF16)
        timed = row_rms(stream, norm_ref[...]).astype(BF16)
        stream_ref[f] = stream
        if not spots:
            timed_refs[0][f] = timed
        elif len(timed_refs) == 1:
            for k in range(part // spots):
                timed_refs[0][(k * frames + f) * spots : (k * frames + f + 1) * spots] = timed[k * spots : (k + 1) * spots]
        else:
            timed_buf[...] = timed
            for k, ref in enumerate(timed_refs):
                ref[f * spots : (f + 1) * spots] = timed_buf[at((me_ref[0] ^ k) * spots, spots), :]


def time_kernel(head, frames_here, spots, pieces, me_ref, gain_ref, wkv_ref, wq_ref, *refs):
    x_refs, out_refs, (q_buf, k_buf, v_buf, bias, att) = refs[:pieces], refs[pieces : 2 * pieces], refs[2 * pieces :]
    x = jnp.concatenate([ref[...] for ref in x_refs], axis=0)
    rows = x.shape[0]
    step = rows // pieces
    half = wkv_ref.shape[1] // 2
    kv_heads = half // head
    group, wide = wq_ref.shape[1] // head // kv_heads, 2 * head

    def place(axis):
        n = lax.broadcasted_iota(jnp.int32, (rows, rows), axis)
        source = n // (frames_here * spots)
        return (source ^ me_ref[0]) * frames_here + (n // spots) % frames_here, n % spots

    (frame_k, spot_k), (frame_q, spot_q) = place(0), place(1)
    bias[...] = jnp.where((spot_q == spot_k) & (frame_q >= frame_k), 0.0, -1e30)
    kv = dot(x, wkv_ref[...]).T
    k_buf[...] = feature_rms(kv[:half], column(gain_ref[1:2, :])).T.astype(BF16)
    v_buf[...] = kv[half:].astype(BF16)
    q = feature_rms(dot(x, wq_ref[...]).T, column(gain_ref[0:1, :]))
    q_buf[...] = (q.astype(BF16).astype(F32) * head**-0.5).astype(BF16)
    for g in range(kv_heads):
        keys = k_buf[:, (g // 2) * wide : (g // 2 + 1) * wide]
        s = dot(keys, query_columns(q_buf, (), g, group, head, g % 2 == 1))
        s = jnp.concatenate([s[:, i * rows : (i + 1) * rows] + bias[...] for i in range(group)], axis=1)
        largest = jnp.max(s, axis=0, keepdims=True)
        e = jnp.exp2((s - largest) * LOG2E)
        total = jnp.sum(e, axis=0, keepdims=True)
        out = (dot(v_buf[g * head : (g + 1) * head], e.astype(BF16)) / total).astype(BF16)
        for i in range(group):
            h = g * group + i
            att[h * head : (h + 1) * head] = out[:, i * rows : (i + 1) * rows]
    out = att[...].T
    for i, ref in enumerate(out_refs):
        ref[...] = out[i * step : (i + 1) * step]


def final_kernel(first, spots, pieces, me_ref, x_ref, w_ref, *refs):
    a_refs, (out_hbm, a_buf, out_buf, sem) = refs[:pieces], refs[-4:]
    frames, part = x_ref.shape[0], x_ref.shape[1]
    copies = []
    for f in range(frames):
        if not spots:
            a_buf[...] = a_refs[0][f]
        else:
            for k in range(part // spots):
                start = f * spots if pieces > 1 else (k * frames + f) * spots
                a_buf[at((me_ref[0] ^ k) * spots, spots), :] = a_refs[k if pieces > 1 else 0][start : start + spots]
        out_buf[f] = (x_ref[f].astype(F32) + dot(a_buf[...], w_ref[...])).astype(BF16)
        copies.append(pltpu.make_async_copy(out_buf.at[f], out_hbm.at[f, pl.ds(first, part)], sem.at[f]))
        copies[-1].start()
    for copy in copies:
        copy.wait()


def size_of(arrays):
    return sum(a.size * a.dtype.itemsize for a in arrays)


def call(kernel, args, outs, flops, scratch=(), anywhere=(), out_anywhere=False, alias={}, smem=(), room=None):
    vmem = pl.BlockSpec(memory_space=pltpu.VMEM)
    in_specs = [vmem] * len(args)
    for i in anywhere:
        in_specs[i] = pl.BlockSpec(memory_space=pl.ANY)
    for i in smem:
        in_specs[i] = pl.BlockSpec(memory_space=pltpu.SMEM)
    if room is None:
        kept = sum(math.prod(s.shape) * jnp.dtype(s.dtype).itemsize for s in scratch if s.dtype in (BF16, F32))
        room = kept + size_of(a for i, a in enumerate(args) if i not in anywhere) + size_of(outs) + (6 << 20)
    return pl.pallas_call(
        kernel,
        out_shape=outs,
        in_specs=in_specs,
        out_specs=[pl.BlockSpec(memory_space=pl.ANY) if out_anywhere else vmem] * len(outs),
        scratch_shapes=list(scratch),
        input_output_aliases=alias,
        compiler_params=pltpu.CompilerParams(vmem_limit_bytes=room),
        cost_estimate=pl.CostEstimate(flops=int(flops), bytes_accessed=int(size_of(args) + size_of(outs)), transcendentals=0),
    )(*args)


PIECES = (lambda n: n, lambda n: n)


def shaped(*dims, dtype=BF16):
    return jax.ShapeDtypeStruct(dims, dtype)


def permuted(x, axis, size, bit):
    return lax.ppermute(x, axis, [(i, i ^ bit) for i in range(size)])


def make_body(mesh):
    frame_devices, band_devices = mesh.shape["frames"], mesh.shape["band"]
    chunks = 2

    def body(tokens, norm_space, query_space, keyval_space, out_space, qk_space, norm_time, query_time, keyval_time, out_time, qk_time):
        frames, rows, width = tokens.shape
        head = qk_space.shape[1]
        q_width, half = query_space.shape[1], keyval_space.shape[1] // 2
        heads = q_width // head
        flat, part = frames * rows, rows // chunks
        spots = part // frame_devices
        aligned = spots if spots % 16 == 0 else 0
        norm_space, norm_time = norm_space[None], norm_time[None]
        zero = jnp.zeros((1,), jnp.int32)
        index = lax.axis_index("frames").astype(jnp.int32).reshape(1)

        normed, kv = call(
            keyval_kernel,
            (index, tokens.reshape(flat, width), norm_space, keyval_space, qk_space),
            [shaped(flat, width), shaped(frames, rows + half, half)],
            4 * flat * width * half,
            smem=(0,),
        )
        top = band_devices // 2
        far = [permuted(kv, "band", band_devices, top)]
        near, bit = [kv], top // 2
        while bit:
            near += [permuted(p, "band", band_devices, bit) for p in near]
            far += [permuted(p, "band", band_devices, bit) for p in far]
            bit //= 2

        near_keys = rows * len(near)
        outs = call(
            functools.partial(near_kernel, head, chunks, len(near)),
            (normed, query_space, qk_space, *near),
            [shaped(frames, q_width, part)] * chunks
            + [shaped(frames, q_width, part, dtype=F32)] * chunks
            + [shaped(frames, 2 * heads, part, dtype=F32)] * chunks,
            2 * flat * width * q_width + 8 * flat * near_keys * q_width,
            [pltpu.VMEM((frames, q_width, rows), BF16)] + [pltpu.VMEM((near_keys, rows * (q_width // half)), F32)] * 2,
        )
        far_keys = rows * len(far)
        n = frame_devices * frames * spots

        def exchange(xs):
            if len(xs) > 1:
                return [xs[0]] + [permuted(x, "frames", frame_devices, k) for k, x in enumerate(xs) if k]
            return [lax.all_to_all(xs[0].reshape(frame_devices, frames, spots, -1), "frames", 0, 0).reshape(n, -1)]

        streams, sent = [], []
        for c in range(chunks):
            pieces = PIECES[c](frame_devices) if aligned else 1
            stream, *timed = call(
                functools.partial(far_kernel, head, c * part, aligned, len(far)),
                (index if pieces > 1 else zero, outs[c], outs[chunks + c], outs[2 * chunks + c], tokens, norm_time, out_space, *far),
                [shaped(frames, part, width)] + ([shaped(n // pieces, width)] * pieces if aligned else [shaped(frames, part, width)]),
                frames * part * (8 * far_keys * q_width + 2 * q_width * width),
                [pltpu.VMEM((frames, q_width, part), BF16)]
                + [pltpu.VMEM((far_keys, part * (q_width // half)), F32)] * 2
                + [pltpu.VMEM((part, width), BF16)],
                smem=(0,),
            )
            if not aligned:
                timed = [timed[0].reshape(frames, frame_devices, spots, width).swapaxes(0, 1)]
            moved = exchange(timed)
            streams.append(stream)
            sent.append(moved)
        mixed = None
        for c in range(chunks):
            pieces = len(sent[c])
            me = index if pieces > 1 else zero
            atts = call(
                functools.partial(time_kernel, head, frames, spots, pieces),
                (me, qk_time, keyval_time, query_time, *sent[c]),
                [shaped(n // pieces, q_width)] * pieces,
                2 * n * width * (q_width + 2 * half) + 16 * n * n * q_width,
                [
                    pltpu.VMEM((q_width, n), BF16),
                    pltpu.VMEM((n, half), BF16),
                    pltpu.VMEM((half, n), BF16),
                    pltpu.VMEM((n, n), F32),
                    pltpu.VMEM((q_width, n), BF16),
                ],
                smem=(0,),
            )
            back = exchange(atts)
            if not aligned:
                back = [back[0].reshape(frame_devices, frames, spots, q_width).swapaxes(0, 1).reshape(frames, part, q_width)]
            args = (me, streams[c], out_time, *back)
            (mixed,) = call(
                functools.partial(final_kernel, c * part, aligned, pieces),
                args if mixed is None else (*args, mixed),
                [shaped(frames, rows, width)],
                2 * n * width * q_width,
                [pltpu.VMEM((part, q_width), BF16), pltpu.VMEM((frames, part, width), BF16), pltpu.SemaphoreType.DMA((frames,))],
                anywhere=() if mixed is None else (3 + pieces,),
                out_anywhere=True,
                alias={} if mixed is None else {3 + pieces: 0},
                smem=(0,),
            )
        return mixed

    return body


def solution(mesh):
    placed = (P("frames", "band", None),) + (P(),) * 10
    body = make_body(mesh)

    return jax.shard_map(body, mesh=mesh, in_specs=placed, out_specs=P("frames", "band", None), check_vma=False)
```

```python
import functools
import math

import jax
import jax.numpy as jnp
from jax import lax
from jax.experimental import pallas as pl
from jax.experimental.pallas import tpu as pltpu
from jax.sharding import PartitionSpec as P


EPS = 1e-06
LOG2E = 1.4426950408889634
BF16 = jnp.bfloat16
F32 = jnp.float32


def dot(a, b):
    return jnp.dot(a, b, preferred_element_type=F32)


def row_rms(x, gain):
    x = x.astype(F32)
    return x * lax.rsqrt(jnp.mean(x * x, axis=-1, keepdims=True) + EPS) * gain


def column(row):
    n = row.shape[1]
    i = lax.broadcasted_iota(jnp.int32, (n, n), 0)
    j = lax.broadcasted_iota(jnp.int32, (n, n), 1)
    return jnp.sum(jnp.where(i == j, row, 0.0), axis=1, keepdims=True)


def feature_rms(x, gain):
    n = gain.shape[0]
    y = x.reshape(x.shape[0] // n, n, x.shape[1])
    total = jnp.sum(y * y, axis=1, keepdims=True)
    return (y * lax.rsqrt(total * (1.0 / n) + EPS) * gain[None]).reshape(x.shape)


def at(start, size):
    return pl.ds(pl.multiple_of(start, size), size)


def padded(q, odd):
    zero = jnp.zeros_like(q)
    return jnp.concatenate([zero, q] if odd else [q, zero], axis=0)


def query_columns(q_ref, lead, g, group, head, odd, lanes=slice(None)):
    heads = [q_ref[(*lead, at((g * group + i) * head, head), lanes)] for i in range(group)]
    return jnp.concatenate([padded(q, odd) for q in heads], axis=1)


def keyval_kernel(me_ref, x_hbm, norm_hbm, w_hbm, gain_hbm, normed_ref, kv_ref, x_ref, norm_ref, w_ref, gain_ref, sems):
    frames, rows = x_hbm.shape[0], x_hbm.shape[1]
    half = w_ref.shape[1] // 2
    small = [pltpu.make_async_copy(norm_hbm, norm_ref, sems.at[frames]), pltpu.make_async_copy(gain_hbm, gain_ref, sems.at[frames + 1])]
    x_copies = [pltpu.make_async_copy(x_hbm.at[f], x_ref.at[f], sems.at[f]) for f in range(frames)]
    w_copy = pltpu.make_async_copy(w_hbm, w_ref, sems.at[frames + 2])
    for copy in (*small, x_copies[0], w_copy, *x_copies[1:]):
        copy.start()
    for copy in small:
        copy.wait()
    gain = column(gain_ref[1:2, :])
    for f in range(frames):
        x_copies[f].wait()
        part = slice(f * rows, (f + 1) * rows)
        normed = row_rms(x_ref[f], norm_ref[...]).astype(BF16)
        normed_ref[part] = normed
        if f == 0:
            w_copy.wait()
        kv = dot(normed, w_ref[...]).T
        kv_ref[f, :rows] = feature_rms(kv[:half], gain).T.astype(BF16)
        kv_ref[f, rows:] = kv[half:].astype(BF16)


def over_key_heads(frames, kv_heads, score, finish, bufs):
    pairs = kv_heads // 2
    total = frames * pairs

    def split(step):
        return step // pairs, (step % pairs) * 2

    score(0, 0, False, bufs[0])

    def step(n, carry):
        f, g = split(n)
        f_next, g_next = split(jnp.minimum(n + 1, total - 1))
        score(f, g + 1, True, bufs[1])
        finish(f, g, bufs[0])
        score(f_next, g_next, False, bufs[0])
        finish(f, g + 1, bufs[1])
        return carry

    lax.fori_loop(0, total, step, 0)


def near_kernel(head, pieces, x_ref, w_ref, gain_ref, *refs):
    kv_refs, refs = refs[:pieces], refs[pieces:]
    q_ref, o_ref, ml_ref, s0, s1 = refs
    frames, rows = kv_refs[0].shape[0], x_ref.shape[0] // kv_refs[0].shape[0]
    half = kv_refs[0].shape[2]
    heads, kv_heads = w_ref.shape[1] // head, half // head
    group, wide = heads // kv_heads, 2 * head
    gain = column(gain_ref[0:1, :])
    for f in range(frames):
        q = dot(x_ref[f * rows : (f + 1) * rows], w_ref[...]).T
        q_ref[f] = (feature_rms(q, gain).astype(BF16).astype(F32) * head**-0.5).astype(BF16)

    def score(f, g, odd, buf):
        keys = jnp.concatenate([ref[f, :rows, at((g // 2) * wide, wide)] for ref in kv_refs], axis=0)
        buf[...] = dot(keys, query_columns(q_ref, (f,), g, group, head, odd))

    def finish(f, g, buf):
        s = buf[...]
        largest = jnp.max(s, axis=0, keepdims=True)
        e = jnp.exp2((s - largest) * LOG2E)
        total = jnp.sum(e, axis=0, keepdims=True)
        values = jnp.concatenate([ref[f, at(rows + g * head, head), :] for ref in kv_refs], axis=1)
        out = dot(values, e.astype(BF16))
        for i in range(group):
            h = g * group + i
            lanes = slice(i * rows, (i + 1) * rows)
            o_ref[f, at(h * head, head), :] = out[:, lanes]
            ml_ref[f, g, i : i + 1, :] = largest[:, lanes]
            ml_ref[f, g, group + i : group + i + 1, :] = total[:, lanes]

    over_key_heads(frames, kv_heads, score, finish, (s0, s1))


def far_kernel(head, chunk, top, spots, pieces, me_ref, q_ref, o_ref, ml_ref, x_ref, norm_ref, w_ref, *refs):
    kv_refs, stream_ref, refs = refs[:pieces], refs[pieces], refs[pieces + 1 :]
    timed_refs, (att, s0, s1, timed_buf) = refs[:-4], refs[-4:]
    frames, part, half = stream_ref.shape[0], stream_ref.shape[1], kv_refs[0].shape[2]
    rows = kv_refs[0].shape[1] - half
    heads, kv_heads = q_ref.shape[1] // head, half // head
    group, wide = heads // kv_heads, 2 * head
    mine = slice(chunk * part, (chunk + 1) * part)

    def score(f, g, odd, buf):
        keys = jnp.concatenate([ref[f, :rows, at((g // 2) * wide, wide)] for ref in kv_refs], axis=0)
        buf[...] = dot(keys, query_columns(q_ref, (f,), g, group, head, odd, mine))

    def finish(f, g, buf):
        s = buf[...]
        ml = ml_ref[f, g, :, mine]
        before = jnp.concatenate([ml[i : i + 1] for i in range(group)], axis=1)
        total = jnp.concatenate([ml[group + i : group + i + 1] for i in range(group)], axis=1)
        out = jnp.concatenate([o_ref[f, at((g * group + i) * head, head), mine] for i in range(group)], axis=1)
        largest = jnp.maximum(before, jnp.max(s, axis=0, keepdims=True))
        scale = jnp.exp2((before - largest) * LOG2E)
        e = jnp.exp2((s - largest) * LOG2E)
        total = total * scale + jnp.sum(e, axis=0, keepdims=True)
        values = jnp.concatenate([ref[f, at(rows + g * head, head), :] for ref in kv_refs], axis=1)
        out = ((out * scale + dot(values, e.astype(BF16))) / total).astype(BF16)
        for i in range(group):
            att[f, at((g * group + i) * head, head), :] = out[:, i * part : (i + 1) * part]

    over_key_heads(frames, kv_heads, score, finish, (s0, s1))
    for f in range(frames):
        update = dot(att[f].T, w_ref[...])
        stream = (x_ref[f, mine].astype(F32) + update).astype(BF16)
        timed = row_rms(stream, norm_ref[...]).astype(BF16)
        stream_ref[f] = stream
        if not top:
            timed_refs[0][f] = timed
        else:
            timed_buf[...] = timed
            for k, ref in enumerate(timed_refs):
                ref[f * spots : (f + 1) * spots] = timed_buf[at(((me_ref[0] ^ k) % top) * spots, spots), :]


def in_groups(refs, frames, spots, groups):
    sub = spots // groups
    starts = [(p, f * spots + h * sub) for h in range(groups) for p in range(len(refs)) for f in range(frames)]
    return jnp.concatenate([refs[p][start : start + sub] for p, start in starts], axis=0)


def out_of_groups(x, refs, frames, spots, groups):
    sub = spots // groups
    n = 0
    for h in range(groups):
        for ref in refs:
            for f in range(frames):
                ref[f * spots + h * sub : f * spots + (h + 1) * sub] = x[n * sub : (n + 1) * sub]
                n += 1


def project(head, x, gain_ref, wkv_ref, wq_ref, q_ref, kv_ref):
    half = wkv_ref.shape[1] // 2
    kv = dot(x, wkv_ref[...]).T
    kv_ref[: x.shape[0]] = feature_rms(kv[:half], column(gain_ref[1:2, :])).T.astype(BF16)
    kv_ref[x.shape[0] :] = kv[half:].astype(BF16)
    q = feature_rms(dot(x, wq_ref[...]).T, column(gain_ref[0:1, :]))
    q_ref[...] = (q.astype(BF16).astype(F32) * head**-0.5).astype(BF16)


def attend_time(head, q_ref, kv_refs, bias, att, groups):
    count = q_ref.shape[1]
    kv_heads = (kv_refs[0].shape[0] - count) // head
    group, wide, cols = q_ref.shape[0] // head // kv_heads, 2 * head, count // groups
    for h in range(groups):
        lanes = slice(h * cols, (h + 1) * cols)
        for g in range(kv_heads):
            keys = jnp.concatenate([ref[lanes, (g // 2) * wide : (g // 2 + 1) * wide] for ref in kv_refs], axis=0)
            s = dot(keys, query_columns(q_ref, (), g, group, head, g % 2 == 1, lanes))
            s = jnp.concatenate([s[:, i * cols : (i + 1) * cols] + bias[...] for i in range(group)], axis=1)
            largest = jnp.max(s, axis=0, keepdims=True)
            e = jnp.exp2((s - largest) * LOG2E)
            total = jnp.sum(e, axis=0, keepdims=True)
            values = jnp.concatenate([ref[count + g * head : count + (g + 1) * head, lanes] for ref in kv_refs], axis=1)
            out = (dot(values, e.astype(BF16)) / total).astype(BF16)
            for i in range(group):
                att[(g * group + i) * head : (g * group + i + 1) * head, lanes] = out[:, i * cols : (i + 1) * cols]


def causal_bias(bias, frames, sub, me_ref):
    def place(axis):
        n = lax.broadcasted_iota(jnp.int32, bias.shape, axis)
        return (n // (frames * sub) ^ me_ref[0]) * frames + (n // sub) % frames, n % sub

    (frame_k, spot_k), (frame_q, spot_q) = place(0), place(1)
    bias[...] = jnp.where((spot_q == spot_k) & (frame_q >= frame_k), 0.0, -1e30)


def time_project_kernel(head, frames, spots, groups, pieces, gain_ref, wkv_ref, wq_ref, *refs):
    x_refs, (q_ref, kv_ref) = refs[:pieces], refs[pieces:]
    project(head, in_groups(x_refs, frames, spots, groups), gain_ref, wkv_ref, wq_ref, q_ref, kv_ref)


def time_attend_kernel(head, frames, spots, groups, pieces, me_ref, q_ref, kv_ref, kv_other, *refs):
    out_refs, (bias, att) = refs[:pieces], refs[pieces:]
    causal_bias(bias, frames, spots // groups, me_ref)
    attend_time(head, q_ref, (kv_ref, kv_other), bias, att, groups)
    out_of_groups(att[...].T, out_refs, frames, spots, groups)


def time_whole_kernel(head, frames, spots, me_ref, gain_ref, wkv_ref, wq_ref, x_ref, out_ref, q_buf, kv_buf, bias, att):
    causal_bias(bias, frames, spots, me_ref)
    project(head, x_ref[...], gain_ref, wkv_ref, wq_ref, q_buf, kv_buf)
    attend_time(head, q_buf, (kv_buf,), bias, att, 1)
    out_ref[...] = att[...].T


def final_kernel(chunk, top, spots, pieces, me_ref, w_ref, x_ref, *refs):
    a_refs, (out_hbm, a_buf, out_buf, sem) = refs[:pieces], refs[-4:]
    frames, part = x_ref.shape[0], x_ref.shape[1]
    copies = []
    for f in range(frames):
        if not top:
            a_buf[...] = a_refs[0][f]
        else:
            for k, ref in enumerate(a_refs):
                a_buf[at(((me_ref[0] ^ k) % top) * spots, spots), :] = ref[f * spots : (f + 1) * spots]
        out_buf[f] = (x_ref[f].astype(F32) + dot(a_buf[...], w_ref[...])).astype(BF16)
        copies.append(pltpu.make_async_copy(out_buf.at[f], out_hbm.at[f, pl.ds(chunk * part, part)], sem.at[f]))
        copies[-1].start()
    for copy in copies:
        copy.wait()


def size_of(arrays):
    return sum(a.size * a.dtype.itemsize for a in arrays)


def call(kernel, args, outs, flops, scratch=(), anywhere=(), out_anywhere=False, alias={}, smem=(), room=None):
    vmem = pl.BlockSpec(memory_space=pltpu.VMEM)
    in_specs = [vmem] * len(args)
    for i in anywhere:
        in_specs[i] = pl.BlockSpec(memory_space=pl.ANY)
    for i in smem:
        in_specs[i] = pl.BlockSpec(memory_space=pltpu.SMEM)
    if room is None:
        kept = sum(math.prod(s.shape) * jnp.dtype(s.dtype).itemsize for s in scratch if s.dtype in (BF16, F32))
        room = kept + size_of(a for i, a in enumerate(args) if i not in anywhere) + size_of(outs) + (6 << 20)
    return pl.pallas_call(
        kernel,
        out_shape=outs,
        in_specs=in_specs,
        out_specs=[pl.BlockSpec(memory_space=pl.ANY) if out_anywhere else vmem] * len(outs),
        scratch_shapes=list(scratch),
        input_output_aliases=alias,
        compiler_params=pltpu.CompilerParams(vmem_limit_bytes=room),
        cost_estimate=pl.CostEstimate(flops=int(flops), bytes_accessed=int(size_of(args) + size_of(outs)), transcendentals=0),
    )(*args)


FIRST_ROOM = 57 << 20


def shaped(*dims, dtype=BF16):
    return jax.ShapeDtypeStruct(dims, dtype)


def permuted(x, axis, size, bit):
    return lax.ppermute(x, axis, [(i, i ^ bit) for i in range(size)])


def make_body(mesh):
    frame_devices, band_devices = mesh.shape["frames"], mesh.shape["band"]
    chunks, groups = 2, 2

    def body(tokens, norm_space, query_space, keyval_space, out_space, qk_space, norm_time, query_time, keyval_time, out_time, qk_time):
        frames, rows, width = tokens.shape
        head = qk_space.shape[1]
        q_width, half = query_space.shape[1], keyval_space.shape[1] // 2
        flat, part = frames * rows, rows // chunks
        top = frame_devices // 2
        spots = part // top
        n = frames * part
        by_partner = spots % (16 * groups) == 0 and n == half
        top = top if by_partner else 0
        norm_space, norm_time = norm_space[None], norm_time[None]
        index = lax.axis_index("frames").astype(jnp.int32).reshape(1)
        me = index if by_partner else jnp.zeros((1,), jnp.int32)

        normed, kv = call(
            keyval_kernel,
            (index, tokens, norm_space, keyval_space, qk_space),
            [shaped(flat, width), shaped(frames, rows + half, half)],
            4 * flat * width * half,
            [
                pltpu.VMEM(tokens.shape, BF16),
                pltpu.VMEM((1, width), F32),
                pltpu.VMEM(keyval_space.shape, BF16),
                pltpu.VMEM(qk_space.shape, F32),
                pltpu.SemaphoreType.DMA((frames + 3,)),
            ],
            anywhere=(1, 2, 3, 4),
            smem=(0,),
            room=FIRST_ROOM,
        )
        bit = band_devices // 2
        far = [permuted(kv, "band", band_devices, bit)]
        near, bit = [kv], bit // 2
        while bit:
            near += [permuted(p, "band", band_devices, bit) for p in near]
            far += [permuted(p, "band", band_devices, bit) for p in far]
            bit //= 2

        near_keys, far_keys = rows * len(near), rows * len(far)
        state = call(
            functools.partial(near_kernel, head, len(near)),
            (normed, query_space, qk_space, *near),
            [shaped(frames, q_width, rows), shaped(frames, q_width, rows, dtype=F32), shaped(frames, half // head, 2 * q_width // half, rows, dtype=F32)],
            2 * flat * width * q_width + 8 * flat * near_keys * q_width,
            [pltpu.VMEM((near_keys, rows * (q_width // half)), F32)] * 2,
        )

        def far_part(c):
            outs = [shaped(frames * spots, width)] * top if by_partner else [shaped(frames, part, width)]
            return call(
                functools.partial(far_kernel, head, c, top, spots, len(far)),
                (me, *state, tokens, norm_time, out_space, *far),
                [shaped(frames, part, width)] + outs,
                frames * part * (8 * far_keys * q_width + 2 * q_width * width),
                [pltpu.VMEM((frames, q_width, part), BF16)]
                + [pltpu.VMEM((far_keys, part * (q_width // half)), F32)] * 2
                + [pltpu.VMEM((part, width), BF16)],
                smem=(0,),
            )

        def final_part(c, stream, atts, mixed):
            args = (me, out_time, stream, *atts)
            return call(
                functools.partial(final_kernel, c, top, spots, len(atts)),
                args if mixed is None else (*args, mixed),
                [shaped(frames, rows, width)],
                2 * n * width * q_width,
                [pltpu.VMEM((part, q_width), BF16), pltpu.VMEM((frames, part, width), BF16), pltpu.SemaphoreType.DMA((frames,))],
                anywhere=() if mixed is None else (len(args),),
                out_anywhere=True,
                alias={} if mixed is None else {len(args): 0},
                smem=(0,),
            )[0]

        if not by_partner:
            mixed = None
            for c in range(chunks):
                stream, timed = far_part(c)
                sent = timed.reshape(frames, frame_devices, -1, width).swapaxes(0, 1)
                moved = lax.all_to_all(sent, "frames", 0, 0).reshape(n, width)
                (att,) = call(
                    functools.partial(time_whole_kernel, head, frames, part // frame_devices),
                    (me, qk_time, keyval_time, query_time, moved),
                    [shaped(n, q_width)],
                    2 * n * width * (q_width + 2 * half) + 16 * n * n * q_width,
                    [pltpu.VMEM(s, t) for s, t in (((q_width, n), BF16), ((n + half, max(n, half)), BF16), ((n, n), F32), ((q_width, n), BF16))],
                    smem=(0,),
                )
                back = lax.all_to_all(att.reshape(frame_devices, frames, -1, q_width), "frames", 0, 0)
                back = back.swapaxes(0, 1).reshape(frames, part, q_width)
                mixed = final_part(c, stream, [back], mixed)
            return mixed

        def exchange(xs):
            return [permuted(x, "frames", frame_devices, k) if k else x for k, x in enumerate(xs)]

        sub = n // groups
        streams, moved, projected, back = [], [], [], []
        for c in range(chunks):
            stream, *timed = far_part(c)
            streams.append(stream)
            moved.append(exchange(timed))
        for c in range(chunks):
            q, kv_time = call(
                functools.partial(time_project_kernel, head, frames, spots, groups, top),
                (qk_time, keyval_time, query_time, *moved[c]),
                [shaped(q_width, n), shaped(n + half, half)],
                2 * n * width * (q_width + 2 * half),
            )
            projected.append((q, kv_time, permuted(kv_time, "frames", frame_devices, top)))
        for c in range(chunks):
            atts = call(
                functools.partial(time_attend_kernel, head, frames, spots, groups, top),
                (me, *projected[c]),
                [shaped(frames * spots, q_width)] * top,
                16 * n * 2 * sub * q_width,
                [pltpu.VMEM((2 * sub, sub), F32), pltpu.VMEM((q_width, n), BF16)],
                smem=(0,),
            )
            back.append(exchange(atts))
        mixed = None
        for c in range(chunks):
            mixed = final_part(c, streams[c], back[c], mixed)
        return mixed

    return body


def solution(mesh):
    placed = (P("frames", "band", None),) + (P(),) * 10
    body = make_body(mesh)

    return jax.shard_map(body, mesh=mesh, in_specs=placed, out_specs=P("frames", "band", None), check_vma=False)
```

```python
import functools
import math

import jax
import jax.numpy as jnp
from jax import lax
from jax.experimental import pallas as pl
from jax.experimental.pallas import tpu as pltpu
from jax.sharding import PartitionSpec as P


EPS = 1e-06
LOG2E = 1.4426950408889634
BF16 = jnp.bfloat16
F32 = jnp.float32


def dot(a, b):
    return jnp.dot(a, b, preferred_element_type=F32)


def row_rms(x, gain):
    x = x.astype(F32)
    return x * lax.rsqrt(jnp.mean(x * x, axis=-1, keepdims=True) + EPS) * gain


def column(row):
    n = row.shape[1]
    i = lax.broadcasted_iota(jnp.int32, (n, n), 0)
    j = lax.broadcasted_iota(jnp.int32, (n, n), 1)
    return jnp.sum(jnp.where(i == j, row, 0.0), axis=1, keepdims=True)


def feature_rms(x, gain):
    n = gain.shape[0]
    y = x.reshape(x.shape[0] // n, n, x.shape[1])
    total = jnp.sum(y * y, axis=1, keepdims=True)
    return (y * lax.rsqrt(total * (1.0 / n) + EPS) * gain[None]).reshape(x.shape)


def at(start, size):
    return pl.ds(pl.multiple_of(start, size), size)


def padded(q, odd):
    zero = jnp.zeros_like(q)
    return jnp.concatenate([zero, q] if odd else [q, zero], axis=0)


def query_columns(q_ref, lead, g, group, head, odd, lanes=slice(None)):
    heads = [q_ref[(*lead, at((g * group + i) * head, head), lanes)] for i in range(group)]
    return jnp.concatenate([padded(q, odd) for q in heads], axis=1)


def keyval_kernel(me_ref, x_hbm, norm_hbm, w_hbm, gain_hbm, kv_hbm, x_ref, norm_ref, w_ref, gain_ref, kv_ref, sems, out_sems):
    frames, rows = x_hbm.shape[0], x_hbm.shape[1]
    half = w_ref.shape[1] // 2
    small = [pltpu.make_async_copy(norm_hbm, norm_ref, sems.at[frames]), pltpu.make_async_copy(gain_hbm, gain_ref, sems.at[frames + 1])]
    x_copies = [pltpu.make_async_copy(x_hbm.at[f], x_ref.at[f], sems.at[f]) for f in range(frames)]
    w_copy = pltpu.make_async_copy(w_hbm, w_ref, sems.at[frames + 2])
    for copy in (*small, x_copies[0], w_copy, *x_copies[1:]):
        copy.start()
    for copy in small:
        copy.wait()
    gain = column(gain_ref[1:2, :])
    outs = []
    for f in range(frames):
        x_copies[f].wait()
        normed = row_rms(x_ref[f], norm_ref[...]).astype(BF16)
        if f == 0:
            w_copy.wait()
        kv = dot(normed, w_ref[...]).T
        kv_ref[f, :rows] = feature_rms(kv[:half], gain).T.astype(BF16)
        kv_ref[f, rows:] = kv[half:].astype(BF16)
        outs.append(pltpu.make_async_copy(kv_ref.at[f], kv_hbm.at[f], out_sems.at[f]))
        outs[-1].start()
    for copy in outs:
        copy.wait()


def over_key_heads(frames, kv_heads, score, finish, bufs):
    pairs = kv_heads // 2
    total = frames * pairs

    def split(step):
        return step // pairs, (step % pairs) * 2

    score(0, 0, False, bufs[0])

    def half_step(n):
        f, g = split(n)
        score(f, g + 1, True, bufs[1])
        finish(f, g, bufs[0])

    def step(n, carry):
        half_step(n)
        f, g = split(n)
        score(*split(n + 1), False, bufs[0])
        finish(f, g + 1, bufs[1])
        return carry

    lax.fori_loop(0, total - 1, step, 0)
    half_step(total - 1)
    f, g = split(total - 1)
    finish(f, g + 1, bufs[1])


def near_kernel(head, pieces, x_ref, norm_ref, w_ref, gain_ref, *refs):
    kv_refs, refs = refs[:pieces], refs[pieces:]
    q_ref, o_ref, ml_ref, s0, s1 = refs
    frames, rows, half = x_ref.shape[0], x_ref.shape[1], kv_refs[0].shape[2]
    heads, kv_heads = w_ref.shape[1] // head, half // head
    group, wide = heads // kv_heads, 2 * head
    gain = column(gain_ref[0:1, :])
    for f in range(frames):
        q = dot(row_rms(x_ref[f], norm_ref[...]).astype(BF16), w_ref[...]).T
        q_ref[f] = (feature_rms(q, gain).astype(BF16).astype(F32) * head**-0.5).astype(BF16)

    def score(f, g, odd, buf):
        keys = jnp.concatenate([ref[f, :rows, at((g // 2) * wide, wide)] for ref in kv_refs], axis=0)
        buf[...] = dot(keys, query_columns(q_ref, (f,), g, group, head, odd))

    def finish(f, g, buf):
        s = buf[...]
        largest = jnp.max(s, axis=0, keepdims=True)
        e = jnp.exp2((s - largest) * LOG2E)
        total = jnp.sum(e, axis=0, keepdims=True)
        values = jnp.concatenate([ref[f, at(rows + g * head, head), :] for ref in kv_refs], axis=1)
        out = dot(values, e.astype(BF16))
        for i in range(group):
            h = g * group + i
            lanes = slice(i * rows, (i + 1) * rows)
            o_ref[f, at(h * head, head), :] = out[:, lanes]
            ml_ref[f, g, i : i + 1, :] = largest[:, lanes]
            ml_ref[f, g, group + i : group + i + 1, :] = total[:, lanes]

    over_key_heads(frames, kv_heads, score, finish, (s0, s1))


def far_kernel(head, chunk, top, spots, pieces, me_ref, q_ref, o_ref, ml_ref, x_ref, norm_ref, w_ref, *refs):
    kv_refs, stream_ref, refs = refs[:pieces], refs[pieces], refs[pieces + 1 :]
    timed_refs, (att, s0, s1, timed_buf) = refs[:-4], refs[-4:]
    frames, part, half = stream_ref.shape[0], stream_ref.shape[1], kv_refs[0].shape[2]
    rows = kv_refs[0].shape[1] - half
    heads, kv_heads = q_ref.shape[1] // head, half // head
    group, wide = heads // kv_heads, 2 * head
    mine = slice(chunk * part, (chunk + 1) * part)

    def score(f, g, odd, buf):
        keys = jnp.concatenate([ref[f, :rows, at((g // 2) * wide, wide)] for ref in kv_refs], axis=0)
        buf[...] = dot(keys, query_columns(q_ref, (f,), g, group, head, odd, mine))

    def finish(f, g, buf):
        s = buf[...]
        ml = ml_ref[f, g, :, mine]
        before = jnp.concatenate([ml[i : i + 1] for i in range(group)], axis=1)
        total = jnp.concatenate([ml[group + i : group + i + 1] for i in range(group)], axis=1)
        out = jnp.concatenate([o_ref[f, at((g * group + i) * head, head), mine] for i in range(group)], axis=1)
        largest = jnp.maximum(before, jnp.max(s, axis=0, keepdims=True))
        scale = jnp.exp2((before - largest) * LOG2E)
        e = jnp.exp2((s - largest) * LOG2E)
        total = total * scale + jnp.sum(e, axis=0, keepdims=True)
        values = jnp.concatenate([ref[f, at(rows + g * head, head), :] for ref in kv_refs], axis=1)
        out = ((out * scale + dot(values, e.astype(BF16))) / total).astype(BF16)
        for i in range(group):
            att[f, at((g * group + i) * head, head), :] = out[:, i * part : (i + 1) * part]

    over_key_heads(frames, kv_heads, score, finish, (s0, s1))
    for f in range(frames):
        update = dot(att[f].T, w_ref[...])
        stream = (x_ref[f, mine].astype(F32) + update).astype(BF16)
        timed = row_rms(stream, norm_ref[...]).astype(BF16)
        stream_ref[f] = stream
        if not top:
            timed_refs[0][f] = timed
        else:
            timed_buf[...] = timed
            for k, ref in enumerate(timed_refs):
                ref[f * spots : (f + 1) * spots] = timed_buf[at(((me_ref[0] ^ k) % top) * spots, spots), :]


def in_groups(refs, frames, spots, groups):
    sub = spots // groups
    starts = [(p, f * spots + h * sub) for h in range(groups) for p in range(len(refs)) for f in range(frames)]
    return jnp.concatenate([refs[p][start : start + sub] for p, start in starts], axis=0)


def out_of_groups(x, refs, frames, spots, groups):
    sub = spots // groups
    n = 0
    for h in range(groups):
        for ref in refs:
            for f in range(frames):
                ref[f * spots + h * sub : f * spots + (h + 1) * sub] = x[n * sub : (n + 1) * sub]
                n += 1


def project(head, x, gain_ref, wkv_ref, wq_ref, q_ref, kv_ref):
    half = wkv_ref.shape[1] // 2
    kv = dot(x, wkv_ref[...]).T
    kv_ref[: x.shape[0]] = feature_rms(kv[:half], column(gain_ref[1:2, :])).T.astype(BF16)
    kv_ref[x.shape[0] :] = kv[half:].astype(BF16)
    q = feature_rms(dot(x, wq_ref[...]).T, column(gain_ref[0:1, :]))
    q_ref[...] = (q.astype(BF16).astype(F32) * head**-0.5).astype(BF16)


def attend_time(head, q_ref, kv_refs, bias, att, groups):
    count = q_ref.shape[1]
    kv_heads = (kv_refs[0].shape[0] - count) // head
    group, wide, cols = q_ref.shape[0] // head // kv_heads, 2 * head, count // groups
    for h in range(groups):
        lanes = slice(h * cols, (h + 1) * cols)
        for g in range(kv_heads):
            keys = jnp.concatenate([ref[lanes, (g // 2) * wide : (g // 2 + 1) * wide] for ref in kv_refs], axis=0)
            s = dot(keys, query_columns(q_ref, (), g, group, head, g % 2 == 1, lanes))
            s = jnp.concatenate([s[:, i * cols : (i + 1) * cols] + bias[...] for i in range(group)], axis=1)
            largest = jnp.max(s, axis=0, keepdims=True)
            e = jnp.exp2((s - largest) * LOG2E)
            total = jnp.sum(e, axis=0, keepdims=True)
            values = jnp.concatenate([ref[count + g * head : count + (g + 1) * head, lanes] for ref in kv_refs], axis=1)
            out = (dot(values, e.astype(BF16)) / total).astype(BF16)
            for i in range(group):
                att[(g * group + i) * head : (g * group + i + 1) * head, lanes] = out[:, i * cols : (i + 1) * cols]


def causal_bias(bias, frames, sub, me_ref):
    def place(axis):
        n = lax.broadcasted_iota(jnp.int32, bias.shape, axis)
        return (n // (frames * sub) ^ me_ref[0]) * frames + (n // sub) % frames, n % sub

    (frame_k, spot_k), (frame_q, spot_q) = place(0), place(1)
    bias[...] = jnp.where((spot_q == spot_k) & (frame_q >= frame_k), 0.0, -1e30)


def time_project_kernel(head, frames, spots, groups, pieces, gain_ref, wkv_ref, wq_ref, *refs):
    x_refs, (q_ref, kv_ref) = refs[:pieces], refs[pieces:]
    project(head, in_groups(x_refs, frames, spots, groups), gain_ref, wkv_ref, wq_ref, q_ref, kv_ref)


def time_attend_kernel(head, frames, spots, groups, pieces, me_ref, q_ref, kv_ref, kv_other, *refs):
    out_refs, (bias, att) = refs[:pieces], refs[pieces:]
    causal_bias(bias, frames, spots // groups, me_ref)
    attend_time(head, q_ref, (kv_ref, kv_other), bias, att, groups)
    out_of_groups(att[...].T, out_refs, frames, spots, groups)


def time_whole_kernel(head, frames, spots, me_ref, gain_ref, wkv_ref, wq_ref, x_ref, out_ref, q_buf, kv_buf, bias, att):
    causal_bias(bias, frames, spots, me_ref)
    project(head, x_ref[...], gain_ref, wkv_ref, wq_ref, q_buf, kv_buf)
    attend_time(head, q_buf, (kv_buf,), bias, att, 1)
    out_ref[...] = att[...].T


def final_kernel(chunk, top, spots, pieces, me_ref, w_ref, x_ref, *refs):
    a_refs, (out_hbm, a_buf, out_buf, sem) = refs[:pieces], refs[-4:]
    frames, part = x_ref.shape[0], x_ref.shape[1]
    copies = []
    for f in range(frames):
        if not top:
            a_buf[...] = a_refs[0][f]
        else:
            for k, ref in enumerate(a_refs):
                a_buf[at(((me_ref[0] ^ k) % top) * spots, spots), :] = ref[f * spots : (f + 1) * spots]
        out_buf[f] = (x_ref[f].astype(F32) + dot(a_buf[...], w_ref[...])).astype(BF16)
        copies.append(pltpu.make_async_copy(out_buf.at[f], out_hbm.at[f, pl.ds(chunk * part, part)], sem.at[f]))
        copies[-1].start()
    for copy in copies:
        copy.wait()


def size_of(arrays):
    return sum(a.size * a.dtype.itemsize for a in arrays)


def call(kernel, args, outs, flops, scratch=(), anywhere=(), out_anywhere=False, alias={}, smem=(), room=None):
    vmem = pl.BlockSpec(memory_space=pltpu.VMEM)
    in_specs = [vmem] * len(args)
    for i in anywhere:
        in_specs[i] = pl.BlockSpec(memory_space=pl.ANY)
    for i in smem:
        in_specs[i] = pl.BlockSpec(memory_space=pltpu.SMEM)
    if room is None:
        kept = sum(math.prod(s.shape) * jnp.dtype(s.dtype).itemsize for s in scratch if s.dtype in (BF16, F32))
        room = kept + size_of(a for i, a in enumerate(args) if i not in anywhere) + size_of(outs) + (6 << 20)
    return pl.pallas_call(
        kernel,
        out_shape=outs,
        in_specs=in_specs,
        out_specs=[pl.BlockSpec(memory_space=pl.ANY) if out_anywhere else vmem] * len(outs),
        scratch_shapes=list(scratch),
        input_output_aliases=alias,
        compiler_params=pltpu.CompilerParams(vmem_limit_bytes=room),
        cost_estimate=pl.CostEstimate(flops=int(flops), bytes_accessed=int(size_of(args) + size_of(outs)), transcendentals=0),
    )(*args)


FIRST_ROOM = 62976 << 10


def shaped(*dims, dtype=BF16):
    return jax.ShapeDtypeStruct(dims, dtype)


def permuted(x, axis, size, bit):
    return lax.ppermute(x, axis, [(i, i ^ bit) for i in range(size)])


def make_body(mesh):
    frame_devices, band_devices = mesh.shape["frames"], mesh.shape["band"]
    chunks, groups = 2, 2

    def body(tokens, norm_space, query_space, keyval_space, out_space, qk_space, norm_time, query_time, keyval_time, out_time, qk_time):
        frames, rows, width = tokens.shape
        head = qk_space.shape[1]
        q_width, half = query_space.shape[1], keyval_space.shape[1] // 2
        flat, part = frames * rows, rows // chunks
        top = frame_devices // 2
        spots = part // top
        n = frames * part
        by_partner = spots % (16 * groups) == 0 and n == half
        top = top if by_partner else 0
        norm_space, norm_time = norm_space[None], norm_time[None]
        index = lax.axis_index("frames").astype(jnp.int32).reshape(1)
        me = index if by_partner else jnp.zeros((1,), jnp.int32)

        (kv,) = call(
            keyval_kernel,
            (index, tokens, norm_space, keyval_space, qk_space),
            [shaped(frames, rows + half, half)],
            4 * flat * width * half,
            [
                pltpu.VMEM(tokens.shape, BF16),
                pltpu.VMEM((1, width), F32),
                pltpu.VMEM(keyval_space.shape, BF16),
                pltpu.VMEM(qk_space.shape, F32),
                pltpu.VMEM((frames, rows + half, half), BF16),
                pltpu.SemaphoreType.DMA((frames + 3,)),
                pltpu.SemaphoreType.DMA((frames,)),
            ],
            out_anywhere=True,
            anywhere=(1, 2, 3, 4),
            smem=(0,),
            room=FIRST_ROOM,
        )
        bit = band_devices // 2
        far = [permuted(kv, "band", band_devices, bit)]
        near, bit = [kv], bit // 2
        while bit:
            near += [permuted(p, "band", band_devices, bit) for p in near]
            far += [permuted(p, "band", band_devices, bit) for p in far]
            bit //= 2

        near_keys, far_keys = rows * len(near), rows * len(far)
        state = call(
            functools.partial(near_kernel, head, len(near)),
            (tokens, norm_space, query_space, qk_space, *near),
            [shaped(frames, q_width, rows), shaped(frames, q_width, rows, dtype=F32), shaped(frames, half // head, 2 * q_width // half, rows, dtype=F32)],
            2 * flat * width * q_width + 8 * flat * near_keys * q_width,
            [pltpu.VMEM((near_keys, rows * (q_width // half)), F32)] * 2,
        )

        def far_part(c):
            outs = [shaped(frames * spots, width)] * top if by_partner else [shaped(frames, part, width)]
            return call(
                functools.partial(far_kernel, head, c, top, spots, len(far)),
                (me, *state, tokens, norm_time, out_space, *far),
                [shaped(frames, part, width)] + outs,
                frames * part * (8 * far_keys * q_width + 2 * q_width * width),
                [pltpu.VMEM((frames, q_width, part), BF16)]
                + [pltpu.VMEM((far_keys, part * (q_width // half)), F32)] * 2
                + [pltpu.VMEM((part, width), BF16)],
                smem=(0,),
            )

        def final_part(c, stream, atts, mixed):
            args = (me, out_time, stream, *atts)
            return call(
                functools.partial(final_kernel, c, top, spots, len(atts)),
                args if mixed is None else (*args, mixed),
                [shaped(frames, rows, width)],
                2 * n * width * q_width,
                [pltpu.VMEM((part, q_width), BF16), pltpu.VMEM((frames, part, width), BF16), pltpu.SemaphoreType.DMA((frames,))],
                anywhere=() if mixed is None else (len(args),),
                out_anywhere=True,
                alias={} if mixed is None else {len(args): 0},
                smem=(0,),
            )[0]

        if not by_partner:
            mixed = None
            for c in range(chunks):
                stream, timed = far_part(c)
                sent = timed.reshape(frames, frame_devices, -1, width).swapaxes(0, 1)
                moved = lax.all_to_all(sent, "frames", 0, 0).reshape(n, width)
                (att,) = call(
                    functools.partial(time_whole_kernel, head, frames, part // frame_devices),
                    (me, qk_time, keyval_time, query_time, moved),
                    [shaped(n, q_width)],
                    2 * n * width * (q_width + 2 * half) + 16 * n * n * q_width,
                    [pltpu.VMEM(s, t) for s, t in (((q_width, n), BF16), ((n + half, max(n, half)), BF16), ((n, n), F32), ((q_width, n), BF16))],
                    smem=(0,),
                )
                back = lax.all_to_all(att.reshape(frame_devices, frames, -1, q_width), "frames", 0, 0)
                back = back.swapaxes(0, 1).reshape(frames, part, q_width)
                mixed = final_part(c, stream, [back], mixed)
            return mixed

        def exchange(xs):
            return [permuted(x, "frames", frame_devices, k) if k else x for k, x in enumerate(xs)]

        sub = n // groups
        streams, moved, projected, back = [], [], [], []
        for c in range(chunks):
            stream, *timed = far_part(c)
            streams.append(stream)
            moved.append(exchange(timed))
        for c in range(chunks):
            q, kv_time = call(
                functools.partial(time_project_kernel, head, frames, spots, groups, top),
                (qk_time, keyval_time, query_time, *moved[c]),
                [shaped(q_width, n), shaped(n + half, half)],
                2 * n * width * (q_width + 2 * half),
            )
            projected.append((q, kv_time, permuted(kv_time, "frames", frame_devices, top)))
        for c in range(chunks):
            atts = call(
                functools.partial(time_attend_kernel, head, frames, spots, groups, top),
                (me, *projected[c]),
                [shaped(frames * spots, q_width)] * top,
                16 * n * 2 * sub * q_width,
                [pltpu.VMEM((2 * sub, sub), F32), pltpu.VMEM((q_width, n), BF16)],
                smem=(0,),
            )
            back.append(exchange(atts))
        mixed = None
        for c in range(chunks):
            mixed = final_part(c, streams[c], back[c], mixed)
        return mixed

    return body


def solution(mesh):
    placed = (P("frames", "band", None),) + (P(),) * 10
    body = make_body(mesh)

    return jax.shard_map(body, mesh=mesh, in_specs=placed, out_specs=P("frames", "band", None), check_vma=False)
```

```python
import functools
import math

import jax
import jax.numpy as jnp
from jax import lax
from jax.experimental import pallas as pl
from jax.experimental.pallas import tpu as pltpu
from jax.sharding import PartitionSpec as P


EPS = 1e-06
LOG2E = 1.4426950408889634
BF16 = jnp.bfloat16
F32 = jnp.float32


def dot(a, b):
    return jnp.dot(a, b, preferred_element_type=F32)


def row_rms(x, gain):
    x = x.astype(F32)
    return x * lax.rsqrt(jnp.mean(x * x, axis=-1, keepdims=True) + EPS) * gain


def column(row):
    n = row.shape[1]
    i = lax.broadcasted_iota(jnp.int32, (n, n), 0)
    j = lax.broadcasted_iota(jnp.int32, (n, n), 1)
    return jnp.sum(jnp.where(i == j, row, 0.0), axis=1, keepdims=True)


def feature_rms(x, gain):
    n = gain.shape[0]
    y = x.reshape(x.shape[0] // n, n, x.shape[1])
    total = jnp.sum(y * y, axis=1, keepdims=True)
    return (y * lax.rsqrt(total * (1.0 / n) + EPS) * gain[None]).reshape(x.shape)


def at(start, size):
    return pl.ds(pl.multiple_of(start, size), size)


def padded(q, odd):
    zero = jnp.zeros_like(q)
    return jnp.concatenate([zero, q] if odd else [q, zero], axis=0)


def query_columns(q_ref, lead, g, group, head, odd, lanes=slice(None)):
    heads = [q_ref[(*lead, at((g * group + i) * head, head), lanes)] for i in range(group)]
    return jnp.concatenate([padded(q, odd) for q in heads], axis=1)


def keyval_kernel(me_ref, x_hbm, norm_hbm, w_hbm, gain_hbm, kv_hbm, x_ref, norm_ref, w_ref, gain_ref, kv_ref, sems, out_sems):
    frames, rows = x_hbm.shape[0], x_hbm.shape[1]
    half = w_ref.shape[1] // 2
    small = [pltpu.make_async_copy(norm_hbm, norm_ref, sems.at[frames]), pltpu.make_async_copy(gain_hbm, gain_ref, sems.at[frames + 1])]
    x_copies = [pltpu.make_async_copy(x_hbm.at[f], x_ref.at[f], sems.at[f]) for f in range(frames)]
    w_copy = pltpu.make_async_copy(w_hbm, w_ref, sems.at[frames + 2])
    for copy in (*small, x_copies[0], w_copy, *x_copies[1:]):
        copy.start()
    for copy in small:
        copy.wait()
    gain = column(gain_ref[1:2, :])
    outs = []
    for f in range(frames):
        x_copies[f].wait()
        normed = row_rms(x_ref[f], norm_ref[...]).astype(BF16)
        if f == 0:
            w_copy.wait()
        kv = dot(normed, w_ref[...]).T
        kv_ref[f, :rows] = feature_rms(kv[:half], gain).T.astype(BF16)
        kv_ref[f, rows:] = kv[half:].astype(BF16)
        outs.append(pltpu.make_async_copy(kv_ref.at[f], kv_hbm.at[f], out_sems.at[f]))
        outs[-1].start()
    for copy in outs:
        copy.wait()


def over_key_heads(frames, kv_heads, score, finish, bufs):
    pairs = kv_heads // 2
    total = frames * pairs

    def split(step):
        return step // pairs, (step % pairs) * 2

    score(0, 0, False, bufs[0])

    def half_step(n):
        f, g = split(n)
        score(f, g + 1, True, bufs[1])
        finish(f, g, bufs[0])

    def step(n, carry):
        half_step(n)
        f, g = split(n)
        score(*split(n + 1), False, bufs[0])
        finish(f, g + 1, bufs[1])
        return carry

    lax.fori_loop(0, total - 1, step, 0)
    half_step(total - 1)
    f, g = split(total - 1)
    finish(f, g + 1, bufs[1])


def near_kernel(head, pieces, x_ref, norm_ref, w_ref, gain_ref, *refs):
    kv_refs, refs = refs[:pieces], refs[pieces:]
    q_ref, o_ref, ml_ref, s0, s1 = refs
    frames, rows, half = x_ref.shape[0], x_ref.shape[1], kv_refs[0].shape[2]
    heads, kv_heads = w_ref.shape[1] // head, half // head
    group, wide = heads // kv_heads, 2 * head
    gain = column(gain_ref[0:1, :])
    for f in range(frames):
        q = dot(row_rms(x_ref[f], norm_ref[...]).astype(BF16), w_ref[...]).T
        q_ref[f] = (feature_rms(q, gain).astype(BF16).astype(F32) * head**-0.5).astype(BF16)

    def score(f, g, odd, buf):
        keys = jnp.concatenate([ref[f, :rows, at((g // 2) * wide, wide)] for ref in kv_refs], axis=0)
        buf[...] = dot(keys, query_columns(q_ref, (f,), g, group, head, odd))

    def finish(f, g, buf):
        s = buf[...]
        largest = jnp.max(s, axis=0, keepdims=True)
        e = jnp.exp2((s - largest) * LOG2E)
        total = jnp.sum(e, axis=0, keepdims=True)
        values = jnp.concatenate([ref[f, at(rows + g * head, head), :] for ref in kv_refs], axis=1)
        out = dot(values, e.astype(BF16))
        for i in range(group):
            h = g * group + i
            lanes = slice(i * rows, (i + 1) * rows)
            o_ref[f, at(h * head, head), :] = out[:, lanes]
            ml_ref[f, g, i : i + 1, :] = largest[:, lanes]
            ml_ref[f, g, group + i : group + i + 1, :] = total[:, lanes]

    over_key_heads(frames, kv_heads, score, finish, (s0, s1))


def far_kernel(head, chunk, top, spots, pieces, me_ref, q_ref, o_ref, ml_ref, x_ref, norm_ref, w_ref, *refs):
    kv_refs, stream_ref, refs = refs[:pieces], refs[pieces], refs[pieces + 1 :]
    timed_refs, (att, s0, s1, timed_buf) = refs[:-4], refs[-4:]
    frames, part, half = stream_ref.shape[0], stream_ref.shape[1], kv_refs[0].shape[2]
    rows = kv_refs[0].shape[1] - half
    heads, kv_heads = q_ref.shape[1] // head, half // head
    group, wide = heads // kv_heads, 2 * head
    mine = slice(chunk * part, (chunk + 1) * part)

    def score(f, g, odd, buf):
        keys = jnp.concatenate([ref[f, :rows, at((g // 2) * wide, wide)] for ref in kv_refs], axis=0)
        buf[...] = dot(keys, query_columns(q_ref, (f,), g, group, head, odd, mine))

    def finish(f, g, buf):
        s = buf[...]
        ml = ml_ref[f, g, :, mine]
        before = jnp.concatenate([ml[i : i + 1] for i in range(group)], axis=1)
        total = jnp.concatenate([ml[group + i : group + i + 1] for i in range(group)], axis=1)
        out = jnp.concatenate([o_ref[f, at((g * group + i) * head, head), mine] for i in range(group)], axis=1)
        largest = jnp.maximum(before, jnp.max(s, axis=0, keepdims=True))
        scale = jnp.exp2((before - largest) * LOG2E)
        e = jnp.exp2((s - largest) * LOG2E)
        total = total * scale + jnp.sum(e, axis=0, keepdims=True)
        values = jnp.concatenate([ref[f, at(rows + g * head, head), :] for ref in kv_refs], axis=1)
        out = ((out * scale + dot(values, e.astype(BF16))) / total).astype(BF16)
        for i in range(group):
            att[f, at((g * group + i) * head, head), :] = out[:, i * part : (i + 1) * part]

    over_key_heads(frames, kv_heads, score, finish, (s0, s1))
    for f in range(frames):
        update = dot(att[f].T, w_ref[...])
        stream = (x_ref[f, mine].astype(F32) + update).astype(BF16)
        timed = row_rms(stream, norm_ref[...]).astype(BF16)
        stream_ref[f] = stream
        if not top:
            timed_refs[0][f] = timed
        else:
            timed_buf[...] = timed
            for k, ref in enumerate(timed_refs):
                ref[f * spots : (f + 1) * spots] = timed_buf[at(((me_ref[0] ^ k) % top) * spots, spots), :]


def in_groups(refs, frames, spots, groups):
    sub = spots // groups
    starts = [(p, f * spots + h * sub) for h in range(groups) for p in range(len(refs)) for f in range(frames)]
    return jnp.concatenate([refs[p][start : start + sub] for p, start in starts], axis=0)


def out_of_groups(x, refs, frames, spots, groups):
    sub = spots // groups
    n = 0
    for h in range(groups):
        for ref in refs:
            for f in range(frames):
                ref[f * spots + h * sub : f * spots + (h + 1) * sub] = x[n * sub : (n + 1) * sub]
                n += 1


def project(head, x, gain_ref, wkv_ref, wq_ref, q_ref, kv_ref):
    half = wkv_ref.shape[1] // 2
    kv = dot(x, wkv_ref[...]).T
    kv_ref[: x.shape[0]] = feature_rms(kv[:half], column(gain_ref[1:2, :])).T.astype(BF16)
    kv_ref[x.shape[0] :] = kv[half:].astype(BF16)
    q = feature_rms(dot(x, wq_ref[...]).T, column(gain_ref[0:1, :]))
    q_ref[...] = (q.astype(BF16).astype(F32) * head**-0.5).astype(BF16)


def attend_time(head, q_ref, kv_refs, bias, att, groups, before=None, after=None):
    count = q_ref.shape[1]
    kv_heads = (kv_refs[0].shape[0] - count) // head
    group, wide, cols = q_ref.shape[0] // head // kv_heads, 2 * head, count // groups
    for h in range(groups):
        lanes = slice(h * cols, (h + 1) * cols)
        for g in range(kv_heads):
            places = [slice((g * group + i) * head, (g * group + i + 1) * head) for i in range(group)]
            keys = jnp.concatenate([ref[lanes, (g // 2) * wide : (g // 2 + 1) * wide] for ref in kv_refs], axis=0)
            s = dot(keys, query_columns(q_ref, (), g, group, head, g % 2 == 1, lanes))
            s = jnp.concatenate([s[:, i * cols : (i + 1) * cols] + bias[...] for i in range(group)], axis=1)
            largest = jnp.max(s, axis=0, keepdims=True)
            if before is not None:
                ml = before[1][h, g]
                old = jnp.concatenate([ml[i : i + 1] for i in range(group)], axis=1)
                largest = jnp.maximum(largest, old)
                scale = jnp.exp2((old - largest) * LOG2E)
            e = jnp.exp2((s - largest) * LOG2E)
            total = jnp.sum(e, axis=0, keepdims=True)
            values = jnp.concatenate([ref[count + g * head : count + (g + 1) * head, lanes] for ref in kv_refs], axis=1)
            out = dot(values, e.astype(BF16))
            if before is not None:
                total += scale * jnp.concatenate([ml[group + i : group + i + 1] for i in range(group)], axis=1)
                out += scale * jnp.concatenate([before[0][place, lanes] for place in places], axis=1)
            if after is None:
                out = (out / total).astype(BF16)
            for i, place in enumerate(places):
                mine = slice(i * cols, (i + 1) * cols)
                if after is None:
                    att[place, lanes] = out[:, mine]
                else:
                    after[0][place, lanes] = out[:, mine]
                    after[1][h, g, i : i + 1] = largest[:, mine]
                    after[1][h, g, group + i : group + i + 1] = total[:, mine]


def causal_bias(bias, frames, sub, me_ref, first=0):
    def place(axis, first):
        n = lax.broadcasted_iota(jnp.int32, bias.shape, axis)
        return ((n // (frames * sub) + first) ^ me_ref[0]) * frames + (n // sub) % frames, n % sub

    (frame_k, spot_k), (frame_q, spot_q) = place(0, first), place(1, 0)
    bias[...] = jnp.where((spot_q == spot_k) & (frame_q >= frame_k), 0.0, -1e30)


def time_project_kernel(head, frames, spots, groups, pieces, gain_ref, wkv_ref, wq_ref, *refs):
    x_refs, (q_ref, kv_ref) = refs[:pieces], refs[pieces:]
    project(head, in_groups(x_refs, frames, spots, groups), gain_ref, wkv_ref, wq_ref, q_ref, kv_ref)


def time_attend_kernel(head, frames, spots, groups, pieces, me_ref, q_ref, kv_ref, kv_other, *refs):
    out_refs, (bias, att) = refs[:pieces], refs[pieces:]
    causal_bias(bias, frames, spots // groups, me_ref)
    attend_time(head, q_ref, (kv_ref, kv_other), bias, att, groups)
    out_of_groups(att[...].T, out_refs, frames, spots, groups)


def time_own_kernel(head, frames, spots, groups, me_ref, q_ref, kv_ref, o_ref, ml_ref, bias):
    causal_bias(bias, frames, spots // groups, me_ref)
    attend_time(head, q_ref, (kv_ref,), bias, None, groups, after=(o_ref, ml_ref))


def time_other_kernel(head, frames, spots, groups, pieces, me_ref, q_ref, o_ref, ml_ref, kv_other, *refs):
    out_refs, (bias, att) = refs[:pieces], refs[pieces:]
    causal_bias(bias, frames, spots // groups, me_ref, pieces)
    attend_time(head, q_ref, (kv_other,), bias, att, groups, before=(o_ref, ml_ref))
    out_of_groups(att[...].T, out_refs, frames, spots, groups)


def time_whole_kernel(head, frames, spots, me_ref, gain_ref, wkv_ref, wq_ref, x_ref, out_ref, q_buf, kv_buf, bias, att):
    causal_bias(bias, frames, spots, me_ref)
    project(head, x_ref[...], gain_ref, wkv_ref, wq_ref, q_buf, kv_buf)
    attend_time(head, q_buf, (kv_buf,), bias, att, 1)
    out_ref[...] = att[...].T


def final_kernel(chunk, top, spots, pieces, me_ref, w_ref, x_ref, *refs):
    a_refs, (out_hbm, a_buf, out_buf, sem) = refs[:pieces], refs[-4:]
    frames, part = x_ref.shape[0], x_ref.shape[1]
    copies = []
    for f in range(frames):
        if not top:
            a_buf[...] = a_refs[0][f]
        else:
            for k, ref in enumerate(a_refs):
                a_buf[at(((me_ref[0] ^ k) % top) * spots, spots), :] = ref[f * spots : (f + 1) * spots]
        out_buf[f] = (x_ref[f].astype(F32) + dot(a_buf[...], w_ref[...])).astype(BF16)
        copies.append(pltpu.make_async_copy(out_buf.at[f], out_hbm.at[f, pl.ds(chunk * part, part)], sem.at[f]))
        copies[-1].start()
    for copy in copies:
        copy.wait()


def size_of(arrays):
    return sum(a.size * a.dtype.itemsize for a in arrays)


def call(kernel, args, outs, flops, scratch=(), anywhere=(), out_anywhere=False, alias={}, smem=(), room=None):
    vmem = pl.BlockSpec(memory_space=pltpu.VMEM)
    in_specs = [vmem] * len(args)
    for i in anywhere:
        in_specs[i] = pl.BlockSpec(memory_space=pl.ANY)
    for i in smem:
        in_specs[i] = pl.BlockSpec(memory_space=pltpu.SMEM)
    if room is None:
        kept = sum(math.prod(s.shape) * jnp.dtype(s.dtype).itemsize for s in scratch if s.dtype in (BF16, F32))
        room = kept + size_of(a for i, a in enumerate(args) if i not in anywhere) + size_of(outs) + (6 << 20)
    return pl.pallas_call(
        kernel,
        out_shape=outs,
        in_specs=in_specs,
        out_specs=[pl.BlockSpec(memory_space=pl.ANY) if out_anywhere else vmem] * len(outs),
        scratch_shapes=list(scratch),
        input_output_aliases=alias,
        compiler_params=pltpu.CompilerParams(vmem_limit_bytes=room),
        cost_estimate=pl.CostEstimate(flops=int(flops), bytes_accessed=int(size_of(args) + size_of(outs)), transcendentals=0),
    )(*args)


FIRST_ROOM = 62976 << 10


def shaped(*dims, dtype=BF16):
    return jax.ShapeDtypeStruct(dims, dtype)


def permuted(x, axis, size, bit):
    return lax.ppermute(x, axis, [(i, i ^ bit) for i in range(size)])


def make_body(mesh):
    frame_devices, band_devices = mesh.shape["frames"], mesh.shape["band"]
    chunks, groups = 2, 2

    def body(tokens, norm_space, query_space, keyval_space, out_space, qk_space, norm_time, query_time, keyval_time, out_time, qk_time):
        frames, rows, width = tokens.shape
        head = qk_space.shape[1]
        q_width, half = query_space.shape[1], keyval_space.shape[1] // 2
        flat, part = frames * rows, rows // chunks
        top = frame_devices // 2
        spots = part // top
        n = frames * part
        by_partner = spots % (16 * groups) == 0 and n == half
        top = top if by_partner else 0
        norm_space, norm_time = norm_space[None], norm_time[None]
        index = lax.axis_index("frames").astype(jnp.int32).reshape(1)
        me = index if by_partner else jnp.zeros((1,), jnp.int32)

        (kv,) = call(
            keyval_kernel,
            (index, tokens, norm_space, keyval_space, qk_space),
            [shaped(frames, rows + half, half)],
            4 * flat * width * half,
            [
                pltpu.VMEM(tokens.shape, BF16),
                pltpu.VMEM((1, width), F32),
                pltpu.VMEM(keyval_space.shape, BF16),
                pltpu.VMEM(qk_space.shape, F32),
                pltpu.VMEM((frames, rows + half, half), BF16),
                pltpu.SemaphoreType.DMA((frames + 3,)),
                pltpu.SemaphoreType.DMA((frames,)),
            ],
            out_anywhere=True,
            anywhere=(1, 2, 3, 4),
            smem=(0,),
            room=FIRST_ROOM,
        )
        bit = band_devices // 2
        far = [permuted(kv, "band", band_devices, bit)]
        near, bit = [kv], bit // 2
        while bit:
            near += [permuted(p, "band", band_devices, bit) for p in near]
            far += [permuted(p, "band", band_devices, bit) for p in far]
            bit //= 2

        near_keys, far_keys = rows * len(near), rows * len(far)
        state = call(
            functools.partial(near_kernel, head, len(near)),
            (tokens, norm_space, query_space, qk_space, *near),
            [shaped(frames, q_width, rows), shaped(frames, q_width, rows, dtype=F32), shaped(frames, half // head, 2 * q_width // half, rows, dtype=F32)],
            2 * flat * width * q_width + 8 * flat * near_keys * q_width,
            [pltpu.VMEM((near_keys, rows * (q_width // half)), F32)] * 2,
        )

        def far_part(c):
            outs = [shaped(frames * spots, width)] * top if by_partner else [shaped(frames, part, width)]
            return call(
                functools.partial(far_kernel, head, c, top, spots, len(far)),
                (me, *state, tokens, norm_time, out_space, *far),
                [shaped(frames, part, width)] + outs,
                frames * part * (8 * far_keys * q_width + 2 * q_width * width),
                [pltpu.VMEM((frames, q_width, part), BF16)]
                + [pltpu.VMEM((far_keys, part * (q_width // half)), F32)] * 2
                + [pltpu.VMEM((part, width), BF16)],
                smem=(0,),
            )

        def final_part(c, stream, atts, mixed):
            args = (me, out_time, stream, *atts)
            return call(
                functools.partial(final_kernel, c, top, spots, len(atts)),
                args if mixed is None else (*args, mixed),
                [shaped(frames, rows, width)],
                2 * n * width * q_width,
                [pltpu.VMEM((part, q_width), BF16), pltpu.VMEM((frames, part, width), BF16), pltpu.SemaphoreType.DMA((frames,))],
                anywhere=() if mixed is None else (len(args),),
                out_anywhere=True,
                alias={} if mixed is None else {len(args): 0},
                smem=(0,),
            )[0]

        if not by_partner:
            mixed = None
            for c in range(chunks):
                stream, timed = far_part(c)
                sent = timed.reshape(frames, frame_devices, -1, width).swapaxes(0, 1)
                moved = lax.all_to_all(sent, "frames", 0, 0).reshape(n, width)
                (att,) = call(
                    functools.partial(time_whole_kernel, head, frames, part // frame_devices),
                    (me, qk_time, keyval_time, query_time, moved),
                    [shaped(n, q_width)],
                    2 * n * width * (q_width + 2 * half) + 16 * n * n * q_width,
                    [pltpu.VMEM(s, t) for s, t in (((q_width, n), BF16), ((n + half, max(n, half)), BF16), ((n, n), F32), ((q_width, n), BF16))],
                    smem=(0,),
                )
                back = lax.all_to_all(att.reshape(frame_devices, frames, -1, q_width), "frames", 0, 0)
                back = back.swapaxes(0, 1).reshape(frames, part, q_width)
                mixed = final_part(c, stream, [back], mixed)
            return mixed

        def exchange(xs):
            out = [xs[0]]
            for k in range(1, len(xs)):
                out.append(permuted(xs[k], "frames", frame_devices, k))
            return out

        sub = n // groups
        streams, moved, projected, back = [], [], [], []
        for c in range(chunks):
            stream, *timed = far_part(c)
            streams.append(stream)
            moved.append(exchange(timed))
        for c in range(chunks):
            q, kv_time = call(
                functools.partial(time_project_kernel, head, frames, spots, groups, top),
                (qk_time, keyval_time, query_time, *moved[c]),
                [shaped(q_width, n), shaped(n + half, half)],
                2 * n * width * (q_width + 2 * half),
            )
            projected.append((q, kv_time, permuted(kv_time, "frames", frame_devices, top)))
        for c in range(chunks):
            kernel, args, seen = time_attend_kernel, (me, *projected[c]), 2 * sub
            if c == chunks - 1:
                q, own, other = projected[c]
                state = call(
                    functools.partial(time_own_kernel, head, frames, spots, groups),
                    (me, q, own),
                    [shaped(q_width, n, dtype=F32), shaped(groups, half // head, 2 * q_width // half, sub, dtype=F32)],
                    8 * n * 2 * sub * q_width,
                    [pltpu.VMEM((sub, sub), F32)],
                    smem=(0,),
                )
                kernel, args, seen = time_other_kernel, (me, q, *state, other), sub
            atts = call(
                functools.partial(kernel, head, frames, spots, groups, top),
                args,
                [shaped(frames * spots, q_width)] * top,
                8 * n * seen * q_width,
                [pltpu.VMEM((seen, sub), F32), pltpu.VMEM((q_width, n), BF16)],
                smem=(0,),
            )
            back.append(exchange(atts))
        mixed = None
        for c in range(chunks):
            mixed = final_part(c, streams[c], back[c], mixed)
        return mixed

    return body


def solution(mesh):
    placed = (P("frames", "band", None),) + (P(),) * 10
    body = make_body(mesh)

    return jax.shard_map(body, mesh=mesh, in_specs=placed, out_specs=P("frames", "band", None), check_vma=False)
```
